512 devices in a mesh: frame: 16 (over y_hi, z), row: 32 (over y_lo, x, core).
Axes of the slice: x: 4, y: 8 (y_hi: 2, y_lo: 4; y = y_hi * 4 + y_lo), z: 8, core: 2. Of those that a mesh axis runs over, the one named last changes fastest.
Arguments:
- fine: bfloat16 [32, 320, 128, 128], P('frame', None, 'row'), may hold values from -6 to 6
- coarse: bfloat16 [4, 256, 1280], P(None, 'row', 'frame'), may hold values from -6 to 6
- w_qkv: bfloat16 [3, 1280, 1280], P(None, None, 'frame'), may hold values from -0.15625 to 0.15625
- w_out: bfloat16 [1280, 1280], P('frame'), may hold values from -0.15625 to 0.15625
- w_up: bfloat16 [1280, 320], P('frame'), may hold values from -0.15625 to 0.15625
- gain_one: float32 [320], replicated, may hold values from 0.1 to 1.9
- conv_space: bfloat16 [3, 3, 320, 320], replicated, may hold values from -0.109375 to 0.109375
- gain_two: float32 [320], replicated, may hold values from 0.1 to 1.9
- conv_time: bfloat16 [3, 320, 320], replicated, may hold values from -0.1875 to 0.1875
Outputs:
- result: bfloat16 [32, 320, 128, 128], P('frame', None, 'row')
The draws below stay inside these ranges and needn't reach their ends.
All inputs are finite; a program needn't handle non-finite values.
Results may differ from the reference program's by a relative error of at most 0.013.
Values may be sent and summed in bfloat16 or wider, within the bound.
No kernel may reach another device: no remote copies, remote signals or barrier semaphores. Data moves between devices by JAX's collectives and lax.ppermute only.
A program may use at most 64 MiB of HBM per device.

```python
import math
import jax
import jax.numpy as jnp
from jax import lax

C = 320
CC = 1280
HEADS = 16
HD = 80
W = 128
CF = 4
FRAMES = 32
ROWS = 128
CH = 16
CW = 16
CP = 256


def shard_levels(own_key, dims, shards, least, top_value):
    def one(dim, parts):
        draws = jax.random.uniform(jax.random.fold_in(jax.random.fold_in(own_key, 6), dim), (parts,), jnp.float32, least / len(shards), top_value / len(shards))
        return jnp.repeat(jnp.exp(draws), dims[dim] // parts).reshape((-1,) + (1,) * (len(dims) - dim - 1))

    loudness = one(*shards[0])
    for cut in shards[1:]:
        loudness = loudness * one(*cut)
    return loudness


def gaussian(rng, shape, scale, most, split=(), held_as=jnp.bfloat16):
    result = scale * jax.random.normal(rng, shape, jnp.float32)
    if split:
        result = result * shard_levels(rng, shape, split, -0.22, 0.18)
    return jnp.clip(result, -most, most).astype(held_as)


def setup_inputs(seed: int = 0) -> dict:
    seeds = jax.random.split(jax.random.key(seed), 10)
    return {
        "fine": gaussian(seeds[0], (FRAMES, C, ROWS, W), 1.0, 6.0, ((0, 16), (2, 32))),
        "coarse": gaussian(seeds[1], (CF, CP, CC), 1.0, 6.0, ((1, 32), (2, 16))),
        "w_qkv": gaussian(seeds[2], (3, CC, CC), CC ** -0.5, 0.15625, ((2, 16),)),
        "w_out": gaussian(seeds[3], (CC, CC), CC ** -0.5, 0.15625, ((0, 16),)),
        "w_up": gaussian(seeds[4], (CC, C), CC ** -0.5, 0.15625, ((0, 16),)),
        "gain_one": jnp.clip(1.0 + 0.18 * jax.random.normal(seeds[5], (C,), jnp.float32), 0.1, 1.9),
        "conv_space": gaussian(seeds[6], (3, 3, C, C), (9 * C) ** -0.5, 0.109375),
        "gain_two": jnp.clip(1.0 + 0.18 * jax.random.normal(seeds[7], (C,), jnp.float32), 0.1, 1.9),
        "conv_time": gaussian(seeds[8], (3, C, C), (3 * C) ** -0.5, 0.1875),
    }


def norm_silu(values, gain):
    square = lax.optimization_barrier(jnp.mean(values * values, axis=-3, keepdims=True))
    scaled = values * lax.rsqrt(square + 1e-06) * gain[:, None, None]
    return jax.nn.silu(scaled).astype(jnp.bfloat16)

def reference(fine, coarse, w_qkv, w_out, w_up, gain_one, conv_space, gain_two, conv_time):
    qkv = jnp.einsum('fpc,icd->ifpd', coarse.astype(jnp.float32), w_qkv.astype(jnp.float32)).astype(jnp.bfloat16)
    query = qkv[0].reshape(CF, CP, HEADS, HD).astype(jnp.float32)
    keys = qkv[1].reshape(CF, CP, HEADS, HD).astype(jnp.float32)
    values = qkv[2].reshape(CF, CP, HEADS, HD).astype(jnp.float32)
    scores = jnp.einsum('fphd,gphd->phfg', query, keys) / math.sqrt(HD)
    probs = jax.nn.softmax(scores, axis=-1).astype(jnp.bfloat16)
    attn = jnp.einsum('phfg,gphd->fphd', probs.astype(jnp.float32), values).astype(jnp.bfloat16).reshape(CF * CP, CC)
    projected = jnp.dot(attn, w_out, preferred_element_type=jnp.float32)
    coarse_out = (coarse.reshape(CF * CP, CC).astype(jnp.float32) + projected).astype(jnp.bfloat16)
    upward = jnp.dot(coarse_out, w_up, preferred_element_type=jnp.float32).astype(jnp.bfloat16)
    upward = upward.reshape(CF, CH, CW, C)

    def first_half(index):
        coarse_frame = (index * CF // FRAMES).astype(jnp.int32)
        cells = lax.dynamic_index_in_dim(upward, coarse_frame, 0, keepdims=False)
        spread = jnp.repeat(jnp.repeat(cells, 8, axis=0), 8, axis=1)
        spread = jnp.transpose(spread, (2, 0, 1)).astype(jnp.float32)
        frame_in = lax.dynamic_index_in_dim(fine, index, 0, keepdims=False).astype(jnp.float32)
        merged = (frame_in + spread).astype(jnp.bfloat16)
        first = norm_silu(merged.astype(jnp.float32), gain_one)
        padded = jnp.pad(first.astype(jnp.float32), ((0, 0), (1, 1), (1, 1)))
        spatial = jnp.zeros((C, ROWS, W), jnp.float32)
        for offset_y in range(3):
            for offset_x in range(3):
                window = padded[:, offset_y:offset_y + ROWS, offset_x:offset_x + W]
                spatial = spatial + jnp.einsum('crw,cd->drw', window, conv_space[offset_y, offset_x].astype(jnp.float32))
        return (merged, norm_silu(spatial, gain_two))
    merged_all, second_all = lax.map(first_half, jnp.arange(FRAMES, dtype=jnp.int32))
    padded_time = jnp.pad(second_all, ((1, 1), (0, 0), (0, 0), (0, 0)))

    def second_half(index):
        window = lax.dynamic_slice_in_dim(padded_time, index, 3, 0)
        temporal = jnp.zeros((C, ROWS, W), jnp.float32)
        for offset in range(3):
            temporal = temporal + jnp.einsum('crw,cd->drw', window[offset].astype(jnp.float32), conv_time[offset].astype(jnp.float32))
        merged = lax.dynamic_index_in_dim(merged_all, index, 0, keepdims=False).astype(jnp.float32)
        return (merged + temporal).astype(jnp.bfloat16)
    return lax.map(second_half, jnp.arange(FRAMES, dtype=jnp.int32))
```

```python
import math

import jax
import jax.numpy as jnp
from jax import lax
from jax.experimental import pallas as pl
from jax.sharding import PartitionSpec as P

HD = 80


def send_all(message, axis, count, groups=None):
    copies = jnp.broadcast_to(message[None], (count, *message.shape))
    return lax.all_to_all(copies, axis, 0, 0, tiled=True, axis_index_groups=groups)


def project(both, folded, w_up, wanted):
    cf, cells, width = both.shape[1:]

    def body(both_ref, folded_ref, up_ref, out_ref):
        attn = both_ref[0].reshape(cf * cells, width)
        inputs = both_ref[1].reshape(cf * cells, width)
        partial = lax.dot_general(
            attn, folded_ref[...], (((1,), (1,)), ((), ())), preferred_element_type=jnp.float32
        )
        partial += jnp.dot(inputs, up_ref[...], preferred_element_type=jnp.float32)
        partial = partial.astype(jnp.bfloat16)
        for place, source in enumerate(wanted):
            out_ref[place] = partial[source * cells : (source + 1) * cells]

    return pl.pallas_call(
        body,
        out_shape=jax.ShapeDtypeStruct((len(wanted), cells, w_up.shape[1]), jnp.bfloat16),
        name="project",
    )(both, folded, w_up)


def norm_silu(values, gain):
    square = jnp.mean(values * values, axis=2, keepdims=True)
    scaled = values * lax.rsqrt(square + 1e-06) * gain[None, None, :, None]
    return jax.nn.silu(scaled)


def fine_stage(ext, up, gain_one, conv_space, gain_two, conv_time, valid):
    above, below, before, after = valid
    width = ext.shape[3]
    wide = jnp.repeat(jnp.swapaxes(up, 2, 3).astype(jnp.float32), width // up.shape[2], axis=3)
    spread = jnp.concatenate([wide[:, :1], *([wide[:, 1:2]] * 4), wide[:, 2:]], axis=1)
    merged = (ext.astype(jnp.float32) + spread).astype(jnp.bfloat16)
    first = norm_silu(merged.astype(jnp.float32), gain_one)
    row_mask = jnp.stack([above, *([jnp.ones_like(above)] * 4), below])
    first = (first * row_mask[None, :, None, None]).astype(jnp.bfloat16)
    padded = jnp.pad(first, ((0, 0), (0, 0), (0, 0), (1, 1)))
    spatial = None
    for dy in range(3):
        for dx in range(3):
            term = jnp.einsum(
                "frcw,cd->frdw",
                padded[:, dy : dy + 4, :, dx : dx + width],
                conv_space[dy, dx],
                preferred_element_type=jnp.float32,
            )
            spatial = term if spatial is None else spatial + term
    second = norm_silu(spatial, gain_two)
    frame_mask = jnp.stack([before, jnp.ones_like(before), jnp.ones_like(before), after])
    second = (second * frame_mask[:, None, None, None]).astype(jnp.bfloat16)
    temporal = None
    for k in range(3):
        term = jnp.einsum(
            "frcw,cd->frdw", second[k : k + 2], conv_time[k], preferred_element_type=jnp.float32
        )
        temporal = term if temporal is None else temporal + term
    result = (merged[1:3, 1:5].astype(jnp.float32) + temporal).astype(jnp.bfloat16)
    return jnp.swapaxes(result, 1, 2)


def local(fine, coarse, w_qkv, w_out, w_up, gain_one, conv_space, gain_two, conv_time):
    frames = lax.axis_size("frame")
    rows = lax.axis_size("row")
    frame = lax.axis_index("frame")
    row = lax.axis_index("row")
    even = row % 2 == 0
    cf, cells, c_dev = coarse.shape
    fine_c = w_up.shape[1]
    tokens = cf * cells
    share = 8
    columns = fine_c // share
    groups = [list(range(k, k + share)) for k in range(0, rows, share)]
    partner = [(i, i ^ 1) for i in range(rows)]
    across = [(i, i + 1) for i in range(1, rows - 1, 2)]
    across += [(b, a) for a, b in across]

    up_slice = lax.dynamic_slice_in_dim(w_up, (row % share) * columns, columns, 1)
    message = jnp.concatenate([coarse.reshape(tokens, c_dev), up_slice.T], axis=0)
    arrived = send_all(message, "frame", frames)
    whole = jnp.swapaxes(arrived, 0, 1).reshape(tokens + columns, frames * c_dev)

    folded_slice = jnp.einsum(
        "jk,dk->jd", whole[tokens:], w_out, preferred_element_type=jnp.float32
    ).astype(jnp.bfloat16)
    folded = send_all(folded_slice, "row", share, groups).reshape(fine_c, c_dev)

    heads = w_qkv.shape[2] // HD
    qkv = jnp.einsum("tc,icd->itd", whole[:tokens], w_qkv, preferred_element_type=jnp.float32)
    qkv = qkv.astype(jnp.bfloat16).reshape(3, cf, cells, heads, HD)
    query, keys, values = qkv[0], qkv[1], qkv[2]
    scores = jnp.einsum(
        "fphd,gphd->phfg", query, keys, preferred_element_type=jnp.float32
    ) / math.sqrt(HD)
    probs = jax.nn.softmax(scores, axis=-1).astype(jnp.bfloat16)
    attn = jnp.einsum("phfg,gphd->fphd", probs, values, preferred_element_type=jnp.float32)
    attn = attn.astype(jnp.bfloat16).reshape(cf, cells, heads * HD)

    mine = jnp.stack([attn, coarse])
    other = lax.ppermute(mine, "row", partner)
    both = jnp.concatenate([jnp.where(even, mine, other), jnp.where(even, other, mine)], axis=2)

    per = frames // cf
    wanted = []
    for f in range(frames):
        wanted.append(max(f - 1, 0) // per)
        wanted.append(min(f + 1, frames - 1) // per)
    outgoing = project(both, folded, w_up, wanted).reshape(frames, 2, 2 * cells, fine_c)
    summed = lax.all_to_all(outgoing, "frame", 0, 0, tiled=True)
    up_own = jnp.sum(summed.astype(jnp.float32), axis=0).astype(jnp.bfloat16)
    up_next = lax.ppermute(up_own, "row", across)

    here = jnp.where(frame % per == 0, up_own[1], up_own[0])
    next_here = jnp.where(frame % per == 0, up_next[1], up_next[0])
    own4 = jnp.stack([up_own[0], here, here, up_own[1]])
    next4 = jnp.stack([up_next[0], next_here, next_here, up_next[1]])
    up = jnp.stack([jnp.where(even, next4, own4), own4, jnp.where(even, own4, next4)], axis=1)

    rows_first = jnp.swapaxes(fine, 1, 2)
    ahead = [(i, i + 1) for i in range(frames - 1)]
    back = [(i + 1, i) for i in range(frames - 1)]
    left = lax.ppermute(rows_first[1:], "frame", ahead)
    right = lax.ppermute(rows_first[:1], "frame", back)
    four = jnp.concatenate([left, rows_first, right], axis=0)
    top, bottom = four[:, :1], four[:, 3:]
    in_pair = lax.ppermute(jnp.where(even, bottom, top), "row", partner)
    beyond = lax.ppermute(jnp.where(even, top, bottom), "row", across)
    ext = jnp.concatenate(
        [jnp.where(even, beyond, in_pair), four, jnp.where(even, in_pair, beyond)], axis=1
    )
    valid = (row > 0, row < rows - 1, frame > 0, frame < frames - 1)
    valid = tuple(v.astype(jnp.float32) for v in valid)
    return fine_stage(ext, up, gain_one, conv_space, gain_two, conv_time, valid)


def solution(mesh):
    return jax.shard_map(
        local,
        mesh=mesh,
        in_specs=(
            P("frame", None, "row", None),
            P(None, "row", "frame"),
            P(None, None, "frame"),
            P("frame", None),
            P("frame", None),
            P(),
            P(),
            P(),
            P(),
        ),
        out_specs=P("frame", None, "row", None),
        check_vma=False,
    )
```

```python
import math

import jax
import jax.numpy as jnp
from jax import lax
from jax.experimental import pallas as pl
from jax.experimental.pallas import tpu as pltpu
from jax.sharding import PartitionSpec as P

HD = 80


def send_all(message, axis, count, groups=None):
    copies = jnp.broadcast_to(message[None], (count, *message.shape))
    return lax.all_to_all(copies, axis, 0, 0, tiled=True, axis_index_groups=groups)


def project(both, folded, w_up, wanted):
    cf, cells, width = both.shape[1:]

    def body(both_ref, folded_ref, up_ref, out_ref):
        attn = both_ref[0].reshape(cf * cells, width)
        inputs = both_ref[1].reshape(cf * cells, width)
        partial = lax.dot_general(
            attn, folded_ref[...], (((1,), (1,)), ((), ())), preferred_element_type=jnp.float32
        )
        partial += jnp.dot(inputs, up_ref[...], preferred_element_type=jnp.float32)
        partial = partial.astype(jnp.bfloat16)
        for place, source in enumerate(wanted):
            out_ref[place] = partial[source * cells : (source + 1) * cells]

    return pl.pallas_call(
        body,
        out_shape=jax.ShapeDtypeStruct((len(wanted), cells, w_up.shape[1]), jnp.bfloat16),
        in_specs=[pl.BlockSpec(memory_space=pltpu.VMEM)] * 3,
        out_specs=pl.BlockSpec(memory_space=pltpu.VMEM),
        compiler_params=pltpu.CompilerParams(vmem_limit_bytes=2 * 2**20),
        name="project",
    )(both, folded, w_up)


def fine_kernel(flags, own, left, right, above, below, up_own, up_next, gains, space, time, out, stack, second, merged):
    channels, width = own.shape[2:]
    cells = up_own.shape[1]
    even, first_slot = flags[0] == 1, flags[1] == 1
    valid_above, valid_below = flags[2].astype(jnp.float32), flags[3].astype(jnp.float32)
    valid_before, valid_after = flags[4].astype(jnp.float32), flags[5].astype(jnp.float32)
    across = width // cells
    column = lax.broadcasted_iota(jnp.int32, (cells, width), 1)
    cell = lax.broadcasted_iota(jnp.int32, (cells, width), 0) * across
    expand = ((column >= cell) & (column < cell + across)).astype(jnp.float32).astype(jnp.bfloat16)
    lane = lax.broadcasted_iota(jnp.int32, (channels, width), 1)

    def spread(cells_of):
        return lax.dot_general(cells_of, expand, (((0,), (0,)), ((), ())), preferred_element_type=jnp.float32)

    here = [spread(up_own[i]) for i in range(2)]
    beyond = [spread(up_next[i]) for i in range(2)]

    def by_frame(pair):
        middle = jnp.where(first_slot, pair[1], pair[0])
        return [pair[0], middle, middle, pair[1]]

    here, beyond = by_frame(here), by_frame(beyond)

    def norm(values, gain, scale):
        square = jnp.sum(values * values, axis=0, keepdims=True) * (1.0 / channels)
        inverse = lax.rsqrt(square + 1e-06)
        if scale is not None:
            inverse = inverse * scale
        half = values * inverse * gain
        return half + half * jnp.tanh(half)

    def keep(frame, position, pixels, added, scale):
        total = (pixels.astype(jnp.float32) + added).astype(jnp.bfloat16)
        if frame in (1, 2) and 1 <= position <= 4:
            merged[frame - 1, position - 1] = total
        normed = norm(total.astype(jnp.float32), gains[0], scale)
        before = jnp.where(lane == 0, 0.0, pltpu.roll(normed, 1, 1))
        after = jnp.where(lane == width - 1, 0.0, pltpu.roll(normed, width - 1, 1))
        lanes = pl.ds(width * (frame % 2), width)
        for place, part in enumerate((before, normed, after)):
            stack[frame // 2, position, pl.ds(place * channels, channels), lanes] = part.astype(jnp.bfloat16)

    for pair in range(2):
        for position in range(6):
            for frame in (2 * pair, 2 * pair + 1):
                if position == 0:
                    keep(frame, 0, above[frame, 0], jnp.where(even, beyond[frame], here[frame]), valid_above)
                elif position == 5:
                    keep(frame, 5, below[frame, 0], jnp.where(even, here[frame], beyond[frame]), valid_below)
                else:
                    held = (left.at[0], own.at[0], own.at[1], right.at[0])[frame]
                    keep(frame, position, held[position - 1], here[frame], None)
        for row in range(4):
            window = stack[pair, pl.ds(row, 3)].reshape(9 * channels, 2 * width)
            spatial = jnp.dot(space[...], window, preferred_element_type=jnp.float32)
            for side in range(2):
                frame = 2 * pair + side
                scale = (valid_before, None, None, valid_after)[frame]
                normed = norm(spatial[:, side * width : (side + 1) * width], gains[1], scale)
                second[row // 2, frame, :, pl.ds(width * (row % 2), width)] = normed.astype(jnp.bfloat16)

    for frame in range(2):
        for half in range(2):
            window = second[half, pl.ds(frame, 3)].reshape(3 * channels, 2 * width)
            temporal = jnp.dot(time[...], window, preferred_element_type=jnp.float32)
            for side in range(2):
                row = 2 * half + side
                total = merged[frame, row].astype(jnp.float32) + temporal[:, side * width : (side + 1) * width]
                out[frame, row] = total.astype(jnp.bfloat16)

def fine_stage(flags, own, left, right, above, below, up_own, up_next, gains, space, time):
    channels, width = own.shape[2:]
    vm = pl.BlockSpec(memory_space=pltpu.VMEM)
    return pl.pallas_call(
        fine_kernel,
        out_shape=jax.ShapeDtypeStruct(own.shape, jnp.bfloat16),
        in_specs=[pl.BlockSpec(memory_space=pltpu.SMEM)] + [vm] * 10,
        out_specs=vm,
        scratch_shapes=[
            pltpu.VMEM((2, 6, 3 * channels, 2 * width), jnp.bfloat16),
            pltpu.VMEM((2, 4, channels, 2 * width), jnp.bfloat16),
            pltpu.VMEM((2, 4, channels, width), jnp.bfloat16),
        ],
        compiler_params=pltpu.CompilerParams(vmem_limit_bytes=24 * 2**20),
        name="fine_stage",
    )(flags, own, left, right, above, below, up_own, up_next, gains, space, time)


def local(fine, coarse, w_qkv, w_out, w_up, gain_one, conv_space, gain_two, conv_time):
    frames = lax.axis_size("frame")
    rows = lax.axis_size("row")
    frame = lax.axis_index("frame")
    row = lax.axis_index("row")
    even = row % 2 == 0
    cf, cells, c_dev = coarse.shape
    fine_c = w_up.shape[1]
    tokens = cf * cells
    share = 8
    columns = fine_c // share
    groups = [list(range(k, k + share)) for k in range(0, rows, share)]
    partner = [(i, i ^ 1) for i in range(rows)]
    across = [(i, i + 1) for i in range(1, rows - 1, 2)]
    across += [(b, a) for a, b in across]

    up_slice = lax.dynamic_slice_in_dim(w_up, (row % share) * columns, columns, 1)
    message = jnp.concatenate([coarse.reshape(tokens, c_dev), up_slice.T], axis=0)
    message, fine, conv_space, conv_time, gain_one, gain_two = lax.optimization_barrier(
        (message, fine, conv_space, conv_time, gain_one, gain_two)
    )
    arrived = send_all(message, "frame", frames)

    width = fine.shape[3]
    rows_first = jnp.swapaxes(fine, 1, 2)
    space = jnp.transpose(conv_space, (3, 0, 1, 2)).reshape(fine_c, 9 * fine_c)
    time = jnp.transpose(conv_time, (2, 0, 1)).reshape(fine_c, 3 * fine_c)
    gains = 0.5 * jnp.stack([gain_one, gain_two])
    gains = jnp.broadcast_to(gains[:, :, None], (2, fine_c, width))

    whole = jnp.swapaxes(arrived, 0, 1).reshape(tokens + columns, frames * c_dev)
    folded_slice = jnp.einsum(
        "jk,dk->jd", whole[tokens:], w_out, preferred_element_type=jnp.float32
    ).astype(jnp.bfloat16)
    copies = jnp.broadcast_to(folded_slice[None], (share, columns, c_dev))
    copies, whole, rows_first, gains = lax.optimization_barrier((copies, whole, rows_first, gains))
    folded = lax.all_to_all(copies, "row", 0, 0, tiled=True, axis_index_groups=groups)
    folded = folded.reshape(fine_c, c_dev)

    heads = w_qkv.shape[2] // HD
    qkv = jnp.einsum("tc,icd->itd", whole[:tokens], w_qkv, preferred_element_type=jnp.float32)
    qkv = qkv.astype(jnp.bfloat16).reshape(3, cf, cells, heads, HD)
    query, keys, values = qkv[0], qkv[1], qkv[2]
    scores = jnp.einsum(
        "fphd,gphd->phfg", query, keys, preferred_element_type=jnp.float32
    ) / math.sqrt(HD)
    probs = jax.nn.softmax(scores, axis=-1).astype(jnp.bfloat16)
    attn = jnp.einsum("phfg,gphd->fphd", probs, values, preferred_element_type=jnp.float32)
    attn = attn.astype(jnp.bfloat16).reshape(cf, cells, heads * HD)

    mine = jnp.stack([attn, coarse])
    other = lax.ppermute(mine, "row", partner)
    both = jnp.concatenate([jnp.where(even, mine, other), jnp.where(even, other, mine)], axis=2)

    left = lax.ppermute(rows_first[1:], "frame", [(i, i + 1) for i in range(frames - 1)])
    right = lax.ppermute(rows_first[:1], "frame", [(i + 1, i) for i in range(frames - 1)])

    per = frames // cf
    wanted = []
    for f in range(frames):
        wanted.append(max(f - 1, 0) // per)
        wanted.append(min(f + 1, frames - 1) // per)
    outgoing = project(both, folded, w_up, wanted).reshape(frames, 2, 2 * cells, fine_c)
    summed = lax.all_to_all(outgoing, "frame", 0, 0, tiled=True)
    near = (left, rows_first, right)
    to_pair = jnp.concatenate([jnp.where(even, part[:, 3:], part[:, :1]) for part in near])
    to_next = jnp.concatenate([jnp.where(even, part[:, :1], part[:, 3:]) for part in near])
    to_pair, to_next, _ = lax.optimization_barrier((to_pair, to_next, outgoing))

    from_pair = lax.ppermute(to_pair, "row", partner)
    from_next = lax.ppermute(to_next, "row", across)
    above = jnp.where(even, from_next, from_pair)
    below = jnp.where(even, from_pair, from_next)

    up_own = jnp.sum(summed.astype(jnp.float32), axis=0).astype(jnp.bfloat16)
    up_next = lax.ppermute(up_own, "row", across)
    flags = jnp.stack([even, frame % per == 0, row > 0, row < rows - 1, frame > 0, frame < frames - 1])
    result = fine_stage(
        flags.astype(jnp.int32), rows_first, left, right, above, below, up_own, up_next, gains, space, time
    )
    return jnp.swapaxes(result, 1, 2)


def solution(mesh):
    return jax.shard_map(
        local,
        mesh=mesh,
        in_specs=(
            P("frame", None, "row", None),
            P(None, "row", "frame"),
            P(None, None, "frame"),
            P("frame", None),
            P("frame", None),
            P(),
            P(),
            P(),
            P(),
        ),
        out_specs=P("frame", None, "row", None),
        check_vma=False,
    )
```

```python
import math

import jax
import jax.numpy as jnp
from jax import lax
from jax.experimental import pallas as pl
from jax.experimental.pallas import tpu as pltpu
from jax.sharding import PartitionSpec as P

HD = 80
VMEM = pl.BlockSpec(memory_space=pltpu.VMEM)
ANY = pl.BlockSpec(memory_space=pl.ANY)
HBM = pl.BlockSpec(memory_space=pltpu.HBM)
FREE = pl.CostEstimate(flops=0, bytes_accessed=0, transcendentals=0)


def limit(mib):
    return pltpu.CompilerParams(vmem_limit_bytes=mib * 2**20)


def pack(coarse, w_up, share, count):
    cf, cells, depth = coarse.shape
    columns = w_up.shape[1] // share

    def body(coarse_in, up_in, out_ref, coarse_ref, up_ref, sems):
        moves = [
            pltpu.make_async_copy(coarse_in, coarse_ref, sems.at[0]),
            pltpu.make_async_copy(up_in, up_ref, sems.at[1]),
        ]
        for move in moves:
            move.start()
        for move in moves:
            move.wait()
        first = lax.rem(lax.axis_index("row"), share) * columns
        shape = (columns, w_up.shape[1])
        wanted = lax.broadcasted_iota(jnp.int32, shape, 0) + first
        pick = (lax.broadcasted_iota(jnp.int32, shape, 1) == wanted).astype(jnp.float32)
        rows = lax.dot_general(
            pick.astype(jnp.bfloat16),
            up_ref[...],
            (((1,), (1,)), ((), ())),
            preferred_element_type=jnp.float32,
        ).astype(jnp.bfloat16)
        for place in range(count):
            for frame in range(cf):
                out_ref[place, pl.ds(frame * cells, cells)] = coarse_ref[frame]
            out_ref[place, pl.ds(cf * cells, columns)] = rows

    return pl.pallas_call(
        body,
        out_shape=jax.ShapeDtypeStruct((count, cf * cells + columns, depth), jnp.bfloat16),
        in_specs=[HBM] * 2,
        out_specs=VMEM,
        scratch_shapes=[
            pltpu.VMEM(coarse.shape, coarse.dtype),
            pltpu.VMEM(w_up.shape, w_up.dtype),
            pltpu.SemaphoreType.DMA((2,)),
        ],
        compiler_params=limit(56),
        cost_estimate=FREE,
        name="pack",
    )(coarse, w_up)


def fold(arrived, w_out, tokens, count):
    blocks, rows, depth = arrived.shape
    heads = w_out.shape[0]

    def body(arrived_ref, out_w_ref, out_ref, cells_ref, whole_ref):
        for block in range(blocks):
            whole_ref[:, pl.ds(block * depth, depth)] = arrived_ref[block]
        cells_ref[...] = whole_ref[pl.ds(0, tokens)]
        total = lax.dot_general(
            whole_ref[pl.ds(tokens, rows - tokens)],
            out_w_ref[...],
            (((1,), (1,)), ((), ())),
            preferred_element_type=jnp.float32,
        ).astype(jnp.bfloat16)
        for place in range(count):
            out_ref[place] = total

    return pl.pallas_call(
        body,
        out_shape=(
            jax.ShapeDtypeStruct((count, rows - tokens, heads), jnp.bfloat16),
            jax.ShapeDtypeStruct((tokens, blocks * depth), jnp.bfloat16),
        ),
        in_specs=[VMEM] * 2,
        out_specs=(VMEM, VMEM),
        scratch_shapes=[pltpu.VMEM((rows, blocks * depth), jnp.bfloat16)],
        compiler_params=limit(2),
        cost_estimate=FREE,
        name="fold",
    )(arrived, w_out)


def attend(whole, w_qkv_t, coarse):
    cf, cells, depth = coarse.shape

    def body(whole_ref, w_ref, coarse_ref, out_ref):
        projected = []
        for part in range(3):
            value = lax.dot_general(
                whole_ref[...],
                w_ref[part],
                (((1,), (1,)), ((), ())),
                preferred_element_type=jnp.float32,
            )
            value = value.astype(jnp.bfloat16).astype(jnp.float32)
            projected.append([value[cells * f : cells * (f + 1)] for f in range(cf)])
        query, keys, values = projected
        for f in range(cf):
            scores = [
                jnp.sum(query[f] * keys[g], axis=1, keepdims=True) * (1.0 / math.sqrt(HD))
                for g in range(cf)
            ]
            most = scores[0]
            for score in scores[1:]:
                most = jnp.maximum(most, score)
            weights = [jnp.exp(score - most) for score in scores]
            total = sum(weights[1:], weights[0])
            mixed = None
            for g in range(cf):
                share = (weights[g] / total).astype(jnp.bfloat16).astype(jnp.float32)
                term = share * values[g]
                mixed = term if mixed is None else mixed + term
            out_ref[0, f] = mixed.astype(jnp.bfloat16)
            out_ref[1, f] = coarse_ref[f]

    return pl.pallas_call(
        body,
        out_shape=jax.ShapeDtypeStruct((2, *coarse.shape), jnp.bfloat16),
        in_specs=[VMEM] * 3,
        out_specs=VMEM,
        compiler_params=limit(2),
        cost_estimate=FREE,
        name="attend",
    )(whole, w_qkv_t, coarse)


def project(mine, other, folded, w_up, earlier, wanted):
    cf, cells, width = mine.shape[1:]

    def body(mine_ref, other_ref, folded_ref, up_ref, _, out_ref):
        even = lax.rem(lax.axis_index("row"), 2) == 0

        def through(ref):
            attn = ref[0].reshape(cf * cells, width)
            inputs = ref[1].reshape(cf * cells, width)
            partial = lax.dot_general(
                attn, folded_ref[...], (((1,), (1,)), ((), ())), preferred_element_type=jnp.float32
            )
            return partial + jnp.dot(inputs, up_ref[...], preferred_element_type=jnp.float32)

        own, far = through(mine_ref), through(other_ref)
        first, second = jnp.where(even, own, far), jnp.where(even, far, own)
        for f in range(cf):
            part = slice(cells * f, cells * (f + 1))
            block = jnp.concatenate([first[part], second[part]], axis=0).astype(jnp.bfloat16)
            for place, source in enumerate(wanted):
                if source == f:
                    out_ref[place] = block

    return pl.pallas_call(
        body,
        out_shape=jax.ShapeDtypeStruct((len(wanted), 2 * cells, w_up.shape[1]), jnp.bfloat16),
        in_specs=[VMEM] * 4 + [HBM],
        out_specs=VMEM,
        compiler_params=limit(2),
        cost_estimate=FREE,
        name="project",
    )(mine, other, folded, w_up, earlier)


def edge_rows(left, own, right):
    rows, channels, width = own.shape[1:]

    def body(left_ref, own_ref, right_ref, pair_ref, next_ref, sems):
        odd = lax.rem(lax.axis_index("row"), 2)
        frames = (left_ref.at[0], own_ref.at[0], own_ref.at[1], right_ref.at[0])
        moves = []
        for place, frame in enumerate(frames):
            for side, (out, row) in enumerate(((pair_ref, 1 - odd), (next_ref, odd))):
                moves.append(
                    pltpu.make_async_copy(
                        frame.at[row * (rows - 1)], out.at[place], sems.at[2 * place + side]
                    )
                )
        for move in moves:
            move.start()
        for move in moves:
            move.wait()

    shape = jax.ShapeDtypeStruct((4, channels, width), jnp.bfloat16)
    return pl.pallas_call(
        body,
        out_shape=(shape, shape),
        in_specs=[ANY] * 3,
        out_specs=(ANY, ANY),
        scratch_shapes=[pltpu.SemaphoreType.DMA((8,))],
        compiler_params=limit(1),
        cost_estimate=FREE,
        name="edge_rows",
    )(left, own, right)


def total(summed, earlier):
    def body(summed_ref, *refs):
        result = summed_ref[0].astype(jnp.float32)
        for source in range(1, summed.shape[0]):
            result += summed_ref[source].astype(jnp.float32)
        refs[-1][...] = result.astype(jnp.bfloat16)

    return pl.pallas_call(
        body,
        out_shape=jax.ShapeDtypeStruct(summed.shape[1:], jnp.bfloat16),
        in_specs=[VMEM] + [ANY] * len(earlier),
        out_specs=VMEM,
        compiler_params=limit(2),
        cost_estimate=FREE,
        name="total",
    )(summed, *earlier)


def fine_kernel(
    own, left_in, right_in, pair_in, next_in, up_own, up_next, one_in, two_in, space_in, time_in,
    out, left, right, pair, beyond, space, time, gains, stack, second, merged, sems,
):
    channels, width = own.shape[2:]
    cells = up_own.shape[1]
    row, frame_index = lax.axis_index("row"), lax.axis_index("frame")
    last_row, last_frame = lax.axis_size("row") - 1, lax.axis_size("frame") - 1
    even = lax.rem(row, 2) == 0
    first_slot = lax.rem(frame_index, 4) == 0
    valid_above = (row > 0).astype(jnp.float32)
    valid_below = (row < last_row).astype(jnp.float32)
    valid_before = (frame_index > 0).astype(jnp.float32)
    valid_after = (frame_index < last_frame).astype(jnp.float32)

    moves = []
    halo = ((left_in, left), (right_in, right), (pair_in, pair), (next_in, beyond))
    kernels = ((space_in, space), (time_in, time))
    for place, (source, target) in enumerate((*halo, *kernels)):
        moves.append(pltpu.make_async_copy(source, target, sems.at[place]))
    for move in moves:
        move.start()

    for place, gain in enumerate((one_in, two_in)):
        gains[place] = jnp.broadcast_to(0.5 * gain[...].reshape(1, channels), (width, channels)).T
    gain_one, gain_two = gains.at[0], gains.at[1]

    across = width // cells
    column = lax.broadcasted_iota(jnp.int32, (cells, width), 1)
    cell = lax.broadcasted_iota(jnp.int32, (cells, width), 0) * across
    expand = ((column >= cell) & (column < cell + across)).astype(jnp.float32).astype(jnp.bfloat16)
    lane = lax.broadcasted_iota(jnp.int32, (channels, width), 1)

    def spread(source):
        by_slot = [
            lax.dot_general(
                source[slot], expand, (((0,), (0,)), ((), ())), preferred_element_type=jnp.float32
            )
            for slot in range(2)
        ]
        middle = jnp.where(first_slot, by_slot[1], by_slot[0])
        return [by_slot[0], middle, middle, by_slot[1]]

    def norm(values, gain, scale):
        square = jnp.sum(values * values, axis=0, keepdims=True) * (1.0 / channels)
        inverse = lax.rsqrt(square + 1e-06)
        if scale is not None:
            inverse = inverse * scale
        half = values * inverse * gain[...]
        return half + half * jnp.tanh(half)

    def keep(frame, position, pixels, added, scale):
        total = (pixels.astype(jnp.float32) + added).astype(jnp.bfloat16)
        if frame in (1, 2) and 1 <= position <= 4:
            merged[frame - 1, position - 1] = total
        normed = norm(total.astype(jnp.float32), gain_one, scale)
        before = jnp.where(lane == 0, 0.0, pltpu.roll(normed, 1, 1))
        after = jnp.where(lane == width - 1, 0.0, pltpu.roll(normed, width - 1, 1))
        lanes = pl.ds(width * (frame % 2), width)
        for place, part in enumerate((before, normed, after)):
            stack[frame // 2, position, pl.ds(place * channels, channels), lanes] = part.astype(
                jnp.bfloat16
            )

    here, further = spread(up_own), spread(up_next)
    for position in range(1, 5):
        keep(1, position, own[0, position - 1], here[1], None)
    for move in moves[:4]:
        move.wait()

    def edges(frame):
        near, far = pair[frame], beyond[frame]
        keep(
            frame, 0, jnp.where(even, far, near), jnp.where(even, further[frame], here[frame]), valid_above
        )
        keep(
            frame, 5, jnp.where(even, near, far), jnp.where(even, here[frame], further[frame]), valid_below
        )

    for position in range(1, 5):
        keep(0, position, left[0, position - 1], here[0], None)
    edges(0)
    edges(1)
    moves[4].wait()
    for half in range(2):
        if half == 1:
            for position in range(1, 5):
                keep(2, position, own[1, position - 1], here[2], None)
                keep(3, position, right[0, position - 1], here[3], None)
            edges(2)
            edges(3)
        for row_out in range(4):
            window = stack[half, pl.ds(row_out, 3)].reshape(9 * channels, 2 * width)
            spatial = jnp.dot(space[...], window, preferred_element_type=jnp.float32)
            for side in range(2):
                frame = 2 * half + side
                scale = (valid_before, None, None, valid_after)[frame]
                normed = norm(spatial[:, side * width : (side + 1) * width], gain_two, scale)
                second[row_out // 2, frame, :, pl.ds(width * (row_out % 2), width)] = normed.astype(
                    jnp.bfloat16
                )

    moves[5].wait()
    for frame in range(2):
        for half in range(2):
            window = second[half, pl.ds(frame, 3)].reshape(3 * channels, 2 * width)
            temporal = jnp.dot(time[...], window, preferred_element_type=jnp.float32)
            for side in range(2):
                row_out = 2 * half + side
                total = merged[frame, row_out].astype(jnp.float32)
                total += temporal[:, side * width : (side + 1) * width]
                out[frame, row_out] = total.astype(jnp.bfloat16)


def fine_stage(own, left, right, pair, beyond, up_own, up_next, gain_one, gain_two, space, time):
    channels, width = own.shape[2:]
    bf16 = jnp.bfloat16
    copied = (left, right, pair, beyond, space, time)
    return pl.pallas_call(
        fine_kernel,
        out_shape=jax.ShapeDtypeStruct(own.shape, bf16),
        in_specs=[VMEM] + [HBM] * 4 + [VMEM] * 4 + [HBM] * 2,
        out_specs=VMEM,
        scratch_shapes=[pltpu.VMEM(array.shape, array.dtype) for array in copied]
        + [
            pltpu.VMEM((2, channels, width), jnp.float32),
            pltpu.VMEM((2, 6, 3 * channels, 2 * width), bf16),
            pltpu.VMEM((2, 4, channels, 2 * width), bf16),
            pltpu.VMEM((2, 4, channels, width), bf16),
            pltpu.SemaphoreType.DMA((len(copied),)),
        ],
        compiler_params=limit(28),
        name="fine_stage",
    )(own, left, right, pair, beyond, up_own, up_next, gain_one, gain_two, space, time)


def local(fine, coarse, w_qkv, w_out, w_up, gain_one, conv_space, gain_two, conv_time):
    frames = lax.axis_size("frame")
    rows = lax.axis_size("row")
    cf, cells, c_dev = coarse.shape
    fine_c, width = fine.shape[1], fine.shape[3]
    tokens = cf * cells
    share = 8
    groups = [list(range(k, k + share)) for k in range(0, rows, share)]
    partner = [(i, i ^ 1) for i in range(rows)]
    across = [(i, i + 1) for i in range(1, rows - 1, 2)]
    across += [(b, a) for a, b in across]

    message = pack(coarse, w_up, share, frames)
    arrived = lax.all_to_all(message, "frame", 0, 0, tiled=True)

    rows_first = jnp.swapaxes(fine, 1, 2)
    left = lax.ppermute(rows_first[1:], "frame", [(i, i + 1) for i in range(frames - 1)])
    right = lax.ppermute(rows_first[:1], "frame", [(i + 1, i) for i in range(frames - 1)])
    space = jnp.transpose(conv_space, (3, 0, 1, 2)).reshape(fine_c, 9 * fine_c)
    time = jnp.transpose(conv_time, (2, 0, 1)).reshape(fine_c, 3 * fine_c)

    copies, whole = fold(arrived, w_out, tokens, share)
    folded = lax.all_to_all(copies, "row", 0, 0, tiled=True, axis_index_groups=groups)
    folded = folded.reshape(fine_c, w_out.shape[0])
    mine = attend(whole, jnp.swapaxes(w_qkv, 1, 2), coarse)
    other = lax.ppermute(mine, "row", partner)

    to_pair, to_next = edge_rows(left, rows_first, right)

    per = frames // cf
    wanted = []
    for f in range(frames):
        wanted.append(max(f - 1, 0) // per)
        wanted.append(min(f + 1, frames - 1) // per)
    outgoing = project(mine, other, folded, w_up, to_pair, wanted).reshape(frames, 2, 2 * cells, fine_c)
    summed = lax.all_to_all(outgoing, "frame", 0, 0, tiled=True)

    from_pair = lax.ppermute(to_pair, "row", partner)
    from_next = lax.ppermute(to_next, "row", across)

    up_own = total(summed, (space, time))
    up_next = lax.ppermute(up_own, "row", across)
    result = fine_stage(
        rows_first, left, right, from_pair, from_next, up_own, up_next, gain_one, gain_two, space, time
    )
    return jnp.swapaxes(result, 1, 2)


def solution(mesh):
    return jax.shard_map(
        local,
        mesh=mesh,
        in_specs=(
            P("frame", None, "row", None),
            P(None, "row", "frame"),
            P(None, None, "frame"),
            P("frame", None),
            P("frame", None),
            P(),
            P(),
            P(),
            P(),
        ),
        out_specs=P("frame", None, "row", None),
        check_vma=False,
    )
```

```python
import math

import jax
import jax.numpy as jnp
from jax import lax
from jax.experimental import pallas as pl
from jax.experimental.pallas import tpu as pltpu
from jax.sharding import PartitionSpec as P

HD = 80
VMEM = pl.BlockSpec(memory_space=pltpu.VMEM)
ANY = pl.BlockSpec(memory_space=pl.ANY)
HBM = pl.BlockSpec(memory_space=pltpu.HBM)
FREE = pl.CostEstimate(flops=0, bytes_accessed=0, transcendentals=0)


def limit(mib):
    return pltpu.CompilerParams(vmem_limit_bytes=mib * 2**20)


def pack(coarse, w_up, share, count):
    cf, cells, depth = coarse.shape
    columns = w_up.shape[1] // share

    def body(coarse_in, up_in, out_ref, coarse_ref, up_ref, sems):
        moves = [
            pltpu.make_async_copy(coarse_in, coarse_ref, sems.at[0]),
            pltpu.make_async_copy(up_in, up_ref, sems.at[1]),
        ]
        for move in moves:
            move.start()
        for move in moves:
            move.wait()
        first = lax.rem(lax.axis_index("row"), share) * columns
        shape = (columns, w_up.shape[1])
        wanted = lax.broadcasted_iota(jnp.int32, shape, 0) + first
        pick = (lax.broadcasted_iota(jnp.int32, shape, 1) == wanted).astype(jnp.float32)
        rows = lax.dot_general(
            pick.astype(jnp.bfloat16),
            up_ref[...],
            (((1,), (1,)), ((), ())),
            preferred_element_type=jnp.float32,
        ).astype(jnp.bfloat16)
        for place in range(count):
            for frame in range(cf):
                out_ref[place, pl.ds(frame * cells, cells)] = coarse_ref[frame]
            out_ref[place, pl.ds(cf * cells, columns)] = rows

    return pl.pallas_call(
        body,
        out_shape=jax.ShapeDtypeStruct((count, cf * cells + columns, depth), jnp.bfloat16),
        in_specs=[HBM] * 2,
        out_specs=VMEM,
        scratch_shapes=[
            pltpu.VMEM(coarse.shape, coarse.dtype),
            pltpu.VMEM(w_up.shape, w_up.dtype),
            pltpu.SemaphoreType.DMA((2,)),
        ],
        compiler_params=limit(56),
        cost_estimate=FREE,
        name="pack",
    )(coarse, w_up)


def fold(arrived, w_out, tokens, count):
    blocks, rows, depth = arrived.shape
    heads = w_out.shape[0]

    def body(arrived_ref, out_w_ref, out_ref, cells_ref, whole_ref):
        for block in range(blocks):
            whole_ref[:, pl.ds(block * depth, depth)] = arrived_ref[block]
        cells_ref[...] = whole_ref[pl.ds(0, tokens)]
        total = lax.dot_general(
            whole_ref[pl.ds(tokens, rows - tokens)],
            out_w_ref[...],
            (((1,), (1,)), ((), ())),
            preferred_element_type=jnp.float32,
        ).astype(jnp.bfloat16)
        for place in range(count):
            out_ref[place] = total

    return pl.pallas_call(
        body,
        out_shape=(
            jax.ShapeDtypeStruct((count, rows - tokens, heads), jnp.bfloat16),
            jax.ShapeDtypeStruct((tokens, blocks * depth), jnp.bfloat16),
        ),
        in_specs=[VMEM] * 2,
        out_specs=(VMEM, VMEM),
        scratch_shapes=[pltpu.VMEM((rows, blocks * depth), jnp.bfloat16)],
        compiler_params=limit(2),
        cost_estimate=FREE,
        name="fold",
    )(arrived, w_out)


def attend(whole, w_qkv_t, coarse):
    cf, cells, depth = coarse.shape

    def body(whole_ref, w_ref, coarse_ref, out_ref):
        projected = []
        for part in range(3):
            value = lax.dot_general(
                whole_ref[...],
                w_ref[part],
                (((1,), (1,)), ((), ())),
                preferred_element_type=jnp.float32,
            )
            value = value.astype(jnp.bfloat16).astype(jnp.float32)
            projected.append([value[cells * f : cells * (f + 1)] for f in range(cf)])
        query, keys, values = projected
        for f in range(cf):
            scores = [
                jnp.sum(query[f] * keys[g], axis=1, keepdims=True) * (1.0 / math.sqrt(HD))
                for g in range(cf)
            ]
            most = scores[0]
            for score in scores[1:]:
                most = jnp.maximum(most, score)
            weights = [jnp.exp(score - most) for score in scores]
            total = sum(weights[1:], weights[0])
            mixed = None
            for g in range(cf):
                share = (weights[g] / total).astype(jnp.bfloat16).astype(jnp.float32)
                term = share * values[g]
                mixed = term if mixed is None else mixed + term
            out_ref[0, f] = mixed.astype(jnp.bfloat16)
            out_ref[1, f] = coarse_ref[f]

    return pl.pallas_call(
        body,
        out_shape=jax.ShapeDtypeStruct((2, *coarse.shape), jnp.bfloat16),
        in_specs=[VMEM] * 3,
        out_specs=VMEM,
        compiler_params=limit(2),
        cost_estimate=pl.CostEstimate(flops=10000000000, bytes_accessed=0, transcendentals=0),
        name="attend",
    )(whole, w_qkv_t, coarse)


def project(mine, other, folded, w_up, wanted):
    cf, cells, width = mine.shape[1:]

    def body(mine_ref, other_ref, folded_ref, up_ref, out_ref):
        even = lax.rem(lax.axis_index("row"), 2) == 0

        def through(ref):
            attn = ref[0].reshape(cf * cells, width)
            inputs = ref[1].reshape(cf * cells, width)
            partial = lax.dot_general(
                attn, folded_ref[...], (((1,), (1,)), ((), ())), preferred_element_type=jnp.float32
            )
            return partial + jnp.dot(inputs, up_ref[...], preferred_element_type=jnp.float32)

        own, far = through(mine_ref), through(other_ref)
        first, second = jnp.where(even, own, far), jnp.where(even, far, own)
        for f in range(cf):
            part = slice(cells * f, cells * (f + 1))
            block = jnp.concatenate([first[part], second[part]], axis=0).astype(jnp.bfloat16)
            for place, source in enumerate(wanted):
                if source == f:
                    out_ref[place] = block

    return pl.pallas_call(
        body,
        out_shape=jax.ShapeDtypeStruct((len(wanted), 2 * cells, w_up.shape[1]), jnp.bfloat16),
        in_specs=[VMEM] * 4,
        out_specs=VMEM,
        compiler_params=limit(2),
        cost_estimate=FREE,
        name="project",
    )(mine, other, folded, w_up)


def edge_rows(left, own, right, earlier):
    rows, channels, width = own.shape[1:]

    def body(left_ref, own_ref, right_ref, *refs):
        pair_ref, next_ref, sems = refs[-3:]
        odd = lax.rem(lax.axis_index("row"), 2)
        frames = (left_ref.at[0], own_ref.at[0], own_ref.at[1], right_ref.at[0])
        moves = []
        for place, frame in enumerate(frames):
            for side, (out, row) in enumerate(((pair_ref, 1 - odd), (next_ref, odd))):
                moves.append(
                    pltpu.make_async_copy(
                        frame.at[row * (rows - 1)], out.at[place], sems.at[2 * place + side]
                    )
                )
        for move in moves:
            move.start()
        for move in moves:
            move.wait()

    shape = jax.ShapeDtypeStruct((4, channels, width), jnp.bfloat16)
    return pl.pallas_call(
        body,
        out_shape=(shape, shape),
        in_specs=[ANY] * (3 + len(earlier)),
        out_specs=(ANY, ANY),
        scratch_shapes=[pltpu.SemaphoreType.DMA((8,))],
        compiler_params=limit(1),
        cost_estimate=FREE,
        name="edge_rows",
    )(left, own, right, *earlier)


def total(summed):
    def body(summed_ref, out_ref):
        result = summed_ref[0].astype(jnp.float32)
        for source in range(1, summed.shape[0]):
            result += summed_ref[source].astype(jnp.float32)
        out_ref[...] = result.astype(jnp.bfloat16)

    return pl.pallas_call(
        body,
        out_shape=jax.ShapeDtypeStruct(summed.shape[1:], jnp.bfloat16),
        in_specs=[VMEM],
        out_specs=VMEM,
        compiler_params=limit(2),
        cost_estimate=FREE,
        name="total",
    )(summed)


def fine_kernel(
    own, left_in, right_in, pair_in, next_in, up_own, up_next, one_in, two_in, space_in, time_in,
    out, left, right, pair, beyond, space, time, gains, stack, second, merged, sems,
):
    channels, width = own.shape[2:]
    cells = up_own.shape[1]
    row, frame_index = lax.axis_index("row"), lax.axis_index("frame")
    last_row, last_frame = lax.axis_size("row") - 1, lax.axis_size("frame") - 1
    even = lax.rem(row, 2) == 0
    first_slot = lax.rem(frame_index, 4) == 0
    valid_above = (row > 0).astype(jnp.float32)
    valid_below = (row < last_row).astype(jnp.float32)
    valid_before = (frame_index > 0).astype(jnp.float32)
    valid_after = (frame_index < last_frame).astype(jnp.float32)

    moves = []
    halo = ((left_in, left), (right_in, right), (pair_in, pair), (next_in, beyond))
    kernels = ((space_in, space), (time_in, time))
    for place, (source, target) in enumerate((*halo, *kernels)):
        moves.append(pltpu.make_async_copy(source, target, sems.at[place]))
    for move in moves:
        move.start()

    for place, gain in enumerate((one_in, two_in)):
        gains[place] = jnp.broadcast_to(0.5 * gain[...].reshape(1, channels), (width, channels)).T
    gain_one, gain_two = gains.at[0], gains.at[1]

    across = width // cells
    column = lax.broadcasted_iota(jnp.int32, (cells, width), 1)
    cell = lax.broadcasted_iota(jnp.int32, (cells, width), 0) * across
    expand = ((column >= cell) & (column < cell + across)).astype(jnp.float32).astype(jnp.bfloat16)
    lane = lax.broadcasted_iota(jnp.int32, (channels, width), 1)

    def spread(source):
        by_slot = [
            lax.dot_general(
                source[slot], expand, (((0,), (0,)), ((), ())), preferred_element_type=jnp.float32
            )
            for slot in range(2)
        ]
        middle = jnp.where(first_slot, by_slot[1], by_slot[0])
        return [by_slot[0], middle, middle, by_slot[1]]

    def norm(values, gain, scale):
        square = jnp.sum(values * values, axis=0, keepdims=True) * (1.0 / channels)
        inverse = lax.rsqrt(square + 1e-06)
        if scale is not None:
            inverse = inverse * scale
        half = values * inverse * gain[...]
        return half + half * jnp.tanh(half)

    def keep(frame, position, pixels, added, scale):
        total = (pixels.astype(jnp.float32) + added).astype(jnp.bfloat16)
        if frame in (1, 2) and 1 <= position <= 4:
            merged[frame - 1, position - 1] = total
        normed = norm(total.astype(jnp.float32), gain_one, scale)
        before = jnp.where(lane == 0, 0.0, pltpu.roll(normed, 1, 1))
        after = jnp.where(lane == width - 1, 0.0, pltpu.roll(normed, width - 1, 1))
        lanes = pl.ds(width * (frame % 2), width)
        for place, part in enumerate((before, normed, after)):
            stack[frame // 2, position, pl.ds(place * channels, channels), lanes] = part.astype(
                jnp.bfloat16
            )

    here, further = spread(up_own), spread(up_next)
    for position in range(1, 5):
        keep(1, position, own[0, position - 1], here[1], None)
    for move in moves[:4]:
        move.wait()

    def edges(frame):
        near, far = pair[frame], beyond[frame]
        keep(
            frame, 0, jnp.where(even, far, near), jnp.where(even, further[frame], here[frame]), valid_above
        )
        keep(
            frame, 5, jnp.where(even, near, far), jnp.where(even, here[frame], further[frame]), valid_below
        )

    for position in range(1, 5):
        keep(0, position, left[0, position - 1], here[0], None)
    edges(0)
    edges(1)
    moves[4].wait()
    for half in range(2):
        if half == 1:
            for position in range(1, 5):
                keep(2, position, own[1, position - 1], here[2], None)
                keep(3, position, right[0, position - 1], here[3], None)
            edges(2)
            edges(3)
        for row_out in range(4):
            window = stack[half, pl.ds(row_out, 3)].reshape(9 * channels, 2 * width)
            spatial = jnp.dot(space[...], window, preferred_element_type=jnp.float32)
            for side in range(2):
                frame = 2 * half + side
                scale = (valid_before, None, None, valid_after)[frame]
                normed = norm(spatial[:, side * width : (side + 1) * width], gain_two, scale)
                second[row_out // 2, frame, :, pl.ds(width * (row_out % 2), width)] = normed.astype(
                    jnp.bfloat16
                )

    moves[5].wait()
    for frame in range(2):
        for half in range(2):
            window = second[half, pl.ds(frame, 3)].reshape(3 * channels, 2 * width)
            temporal = jnp.dot(time[...], window, preferred_element_type=jnp.float32)
            for side in range(2):
                row_out = 2 * half + side
                total = merged[frame, row_out].astype(jnp.float32)
                total += temporal[:, side * width : (side + 1) * width]
                out[frame, row_out] = total.astype(jnp.bfloat16)


def fine_stage(own, left, right, pair, beyond, up_own, up_next, gain_one, gain_two, space, time):
    channels, width = own.shape[2:]
    bf16 = jnp.bfloat16
    copied = (left, right, pair, beyond, space, time)
    return pl.pallas_call(
        fine_kernel,
        out_shape=jax.ShapeDtypeStruct(own.shape, bf16),
        in_specs=[VMEM] + [HBM] * 4 + [VMEM] * 4 + [HBM] * 2,
        out_specs=VMEM,
        scratch_shapes=[pltpu.VMEM(array.shape, array.dtype) for array in copied]
        + [
            pltpu.VMEM((2, channels, width), jnp.float32),
            pltpu.VMEM((2, 6, 3 * channels, 2 * width), bf16),
            pltpu.VMEM((2, 4, channels, 2 * width), bf16),
            pltpu.VMEM((2, 4, channels, width), bf16),
            pltpu.SemaphoreType.DMA((len(copied),)),
        ],
        compiler_params=limit(28),
        name="fine_stage",
    )(own, left, right, pair, beyond, up_own, up_next, gain_one, gain_two, space, time)


def local(fine, coarse, w_qkv, w_out, w_up, gain_one, conv_space, gain_two, conv_time):
    frames = lax.axis_size("frame")
    rows = lax.axis_size("row")
    cf, cells, c_dev = coarse.shape
    fine_c, width = fine.shape[1], fine.shape[3]
    tokens = cf * cells
    share = 8
    groups = [list(range(k, k + share)) for k in range(0, rows, share)]
    partner = [(i, i ^ 1) for i in range(rows)]
    across = [(i, i + 1) for i in range(1, rows - 1, 2)]
    across += [(b, a) for a, b in across]

    message = pack(coarse, w_up, share, frames)
    arrived = lax.all_to_all(message, "frame", 0, 0, tiled=True)

    rows_first = jnp.swapaxes(fine, 1, 2)
    left = lax.ppermute(rows_first[1:], "frame", [(i, i + 1) for i in range(frames - 1)])
    right = lax.ppermute(rows_first[:1], "frame", [(i + 1, i) for i in range(frames - 1)])
    space = jnp.transpose(conv_space, (3, 0, 1, 2)).reshape(fine_c, 9 * fine_c)
    time = jnp.transpose(conv_time, (2, 0, 1)).reshape(fine_c, 3 * fine_c)

    copies, whole = fold(arrived, w_out, tokens, share)
    folded = lax.all_to_all(copies, "row", 0, 0, tiled=True, axis_index_groups=groups)
    folded = folded.reshape(fine_c, w_out.shape[0])
    mine = attend(whole, jnp.swapaxes(w_qkv, 1, 2), coarse)
    other = lax.ppermute(mine, "row", partner)

    per = frames // cf
    wanted = []
    for f in range(frames):
        wanted.append(max(f - 1, 0) // per)
        wanted.append(min(f + 1, frames - 1) // per)
    outgoing = project(mine, other, folded, w_up, wanted).reshape(frames, 2, 2 * cells, fine_c)
    summed = lax.all_to_all(outgoing, "frame", 0, 0, tiled=True)

    to_pair, to_next = edge_rows(left, rows_first, right, (outgoing, space, time))
    from_pair = lax.ppermute(to_pair, "row", partner)
    from_next = lax.ppermute(to_next, "row", across)

    up_own = total(summed)
    up_next = lax.ppermute(up_own, "row", across)
    result = fine_stage(
        rows_first, left, right, from_pair, from_next, up_own, up_next, gain_one, gain_two, space, time
    )
    return jnp.swapaxes(result, 1, 2)


def solution(mesh):
    return jax.shard_map(
        local,
        mesh=mesh,
        in_specs=(
            P("frame", None, "row", None),
            P(None, "row", "frame"),
            P(None, None, "frame"),
            P("frame", None),
            P("frame", None),
            P(),
            P(),
            P(),
            P(),
        ),
        out_specs=P("frame", None, "row", None),
        check_vma=False,
    )
```

```python
import math

import jax
import jax.numpy as jnp
from jax import lax
from jax.experimental import pallas as pl
from jax.experimental.pallas import tpu as pltpu
from jax.sharding import PartitionSpec as P

HD = 80
VMEM = pl.BlockSpec(memory_space=pltpu.VMEM)
ANY = pl.BlockSpec(memory_space=pl.ANY)
HBM = pl.BlockSpec(memory_space=pltpu.HBM)
FREE = pl.CostEstimate(flops=0, bytes_accessed=0, transcendentals=0)


def limit(mib):
    return pltpu.CompilerParams(vmem_limit_bytes=mib * 2**20)


def pack(coarse, w_up, share, count):
    cf, cells, depth = coarse.shape
    columns = w_up.shape[1] // share

    def body(coarse_in, up_in, out_ref, coarse_ref, up_ref, sems):
        moves = [
            pltpu.make_async_copy(coarse_in, coarse_ref, sems.at[0]),
            pltpu.make_async_copy(up_in, up_ref, sems.at[1]),
        ]
        for move in moves:
            move.start()
        for move in moves:
            move.wait()
        first = lax.rem(lax.axis_index("row"), share) * columns
        shape = (columns, w_up.shape[1])
        wanted = lax.broadcasted_iota(jnp.int32, shape, 0) + first
        pick = (lax.broadcasted_iota(jnp.int32, shape, 1) == wanted).astype(jnp.float32)
        rows = lax.dot_general(
            pick.astype(jnp.bfloat16),
            up_ref[...],
            (((1,), (1,)), ((), ())),
            preferred_element_type=jnp.float32,
        ).astype(jnp.bfloat16)
        for place in range(count):
            for frame in range(cf):
                out_ref[place, pl.ds(frame * cells, cells)] = coarse_ref[frame]
            out_ref[place, pl.ds(cf * cells, columns)] = rows

    return pl.pallas_call(
        body,
        out_shape=jax.ShapeDtypeStruct((count, cf * cells + columns, depth), jnp.bfloat16),
        in_specs=[HBM] * 2,
        out_specs=VMEM,
        scratch_shapes=[
            pltpu.VMEM(coarse.shape, coarse.dtype),
            pltpu.VMEM(w_up.shape, w_up.dtype),
            pltpu.SemaphoreType.DMA((2,)),
        ],
        compiler_params=limit(56),
        cost_estimate=FREE,
        name="pack",
    )(coarse, w_up)


def fold(arrived, w_out, tokens, count):
    blocks, rows, depth = arrived.shape
    heads = w_out.shape[0]

    def body(arrived_ref, out_w_ref, out_ref, cells_ref, whole_ref):
        for block in range(blocks):
            whole_ref[:, pl.ds(block * depth, depth)] = arrived_ref[block]
        cells_ref[...] = whole_ref[pl.ds(0, tokens)]
        total = lax.dot_general(
            whole_ref[pl.ds(tokens, rows - tokens)],
            out_w_ref[...],
            (((1,), (1,)), ((), ())),
            preferred_element_type=jnp.float32,
        ).astype(jnp.bfloat16)
        for place in range(count):
            out_ref[place] = total

    return pl.pallas_call(
        body,
        out_shape=(
            jax.ShapeDtypeStruct((count, rows - tokens, heads), jnp.bfloat16),
            jax.ShapeDtypeStruct((tokens, blocks * depth), jnp.bfloat16),
        ),
        in_specs=[VMEM] * 2,
        out_specs=(VMEM, VMEM),
        scratch_shapes=[pltpu.VMEM((rows, blocks * depth), jnp.bfloat16)],
        compiler_params=limit(2),
        cost_estimate=FREE,
        name="fold",
    )(arrived, w_out)


def attend(whole, w_qkv_t, coarse):
    cf, cells, depth = coarse.shape

    def body(whole_ref, w_ref, coarse_ref, out_ref):
        projected = []
        for part in range(3):
            value = lax.dot_general(
                whole_ref[...],
                w_ref[part],
                (((1,), (1,)), ((), ())),
                preferred_element_type=jnp.float32,
            )
            value = value.astype(jnp.bfloat16).astype(jnp.float32)
            projected.append([value[cells * f : cells * (f + 1)] for f in range(cf)])
        query, keys, values = projected
        for f in range(cf):
            scores = [
                jnp.sum(query[f] * keys[g], axis=1, keepdims=True) * (1.0 / math.sqrt(HD))
                for g in range(cf)
            ]
            most = scores[0]
            for score in scores[1:]:
                most = jnp.maximum(most, score)
            weights = [jnp.exp(score - most) for score in scores]
            total = sum(weights[1:], weights[0])
            mixed = None
            for g in range(cf):
                share = (weights[g] / total).astype(jnp.bfloat16).astype(jnp.float32)
                term = share * values[g]
                mixed = term if mixed is None else mixed + term
            out_ref[0, f] = mixed.astype(jnp.bfloat16)
            out_ref[1, f] = coarse_ref[f]

    return pl.pallas_call(
        body,
        out_shape=jax.ShapeDtypeStruct((2, *coarse.shape), jnp.bfloat16),
        in_specs=[VMEM] * 3,
        out_specs=VMEM,
        compiler_params=limit(2),
        cost_estimate=pl.CostEstimate(flops=10000000000, bytes_accessed=0, transcendentals=0),
        name="attend",
    )(whole, w_qkv_t, coarse)


def project(mine, other, folded, w_up, wanted):
    cf, cells, width = mine.shape[1:]

    def body(mine_ref, other_ref, folded_ref, up_ref, out_ref):
        even = lax.rem(lax.axis_index("row"), 2) == 0

        def through(ref):
            attn = ref[0].reshape(cf * cells, width)
            inputs = ref[1].reshape(cf * cells, width)
            partial = lax.dot_general(
                attn, folded_ref[...], (((1,), (1,)), ((), ())), preferred_element_type=jnp.float32
            )
            return partial + jnp.dot(inputs, up_ref[...], preferred_element_type=jnp.float32)

        own, far = through(mine_ref), through(other_ref)
        first, second = jnp.where(even, own, far), jnp.where(even, far, own)
        for f in range(cf):
            part = slice(cells * f, cells * (f + 1))
            block = jnp.concatenate([first[part], second[part]], axis=0).astype(jnp.bfloat16)
            for place, source in enumerate(wanted):
                if source == f:
                    out_ref[place] = block

    return pl.pallas_call(
        body,
        out_shape=jax.ShapeDtypeStruct((len(wanted), 2 * cells, w_up.shape[1]), jnp.bfloat16),
        in_specs=[VMEM] * 4,
        out_specs=VMEM,
        compiler_params=limit(2),
        cost_estimate=FREE,
        name="project",
    )(mine, other, folded, w_up)


def edge_rows(left, own, right, earlier):
    rows, channels, width = own.shape[1:]

    def body(left_ref, own_ref, right_ref, *refs):
        pair_ref, next_ref, sems = refs[-3:]
        odd = lax.rem(lax.axis_index("row"), 2)
        frames = (left_ref.at[0], own_ref.at[0], own_ref.at[1], right_ref.at[0])
        moves = []
        for place, frame in enumerate(frames):
            for side, (out, row) in enumerate(((pair_ref, 1 - odd), (next_ref, odd))):
                moves.append(
                    pltpu.make_async_copy(
                        frame.at[row * (rows - 1)], out.at[place], sems.at[2 * place + side]
                    )
                )
        for move in moves:
            move.start()
        for move in moves:
            move.wait()

    shape = jax.ShapeDtypeStruct((4, channels, width), jnp.bfloat16)
    return pl.pallas_call(
        body,
        out_shape=(shape, shape),
        in_specs=[ANY] * (3 + len(earlier)),
        out_specs=(VMEM, VMEM),
        scratch_shapes=[pltpu.SemaphoreType.DMA((8,))],
        compiler_params=limit(2),
        cost_estimate=FREE,
        name="edge_rows",
    )(left, own, right, *earlier)


def total(summed):
    def body(summed_ref, out_ref):
        result = summed_ref[0].astype(jnp.float32)
        for source in range(1, summed.shape[0]):
            result += summed_ref[source].astype(jnp.float32)
        out_ref[...] = result.astype(jnp.bfloat16)

    return pl.pallas_call(
        body,
        out_shape=jax.ShapeDtypeStruct(summed.shape[1:], jnp.bfloat16),
        in_specs=[VMEM],
        out_specs=VMEM,
        compiler_params=limit(2),
        cost_estimate=FREE,
        name="total",
    )(summed)


def fine_kernel(
    own, left_in, right_in, pair_in, next_in, up_own, up_next, one_in, two_in, space, time,
    out, left, right, pair, beyond, gains, stack, second, merged, mixed, turned, sems, out_sems,
):
    channels, width = own.shape[2:]
    cells = up_own.shape[1]
    row, frame_index = lax.axis_index("row"), lax.axis_index("frame")
    last_row, last_frame = lax.axis_size("row") - 1, lax.axis_size("frame") - 1
    even = lax.rem(row, 2) == 0
    first_slot = lax.rem(frame_index, 4) == 0
    valid_above = (row > 0).astype(jnp.float32)
    valid_below = (row < last_row).astype(jnp.float32)
    valid_before = (frame_index > 0).astype(jnp.float32)
    valid_after = (frame_index < last_frame).astype(jnp.float32)

    moves, leaving = [], []
    halo = ((left_in, left), (right_in, right), (pair_in, pair), (next_in, beyond))
    for place, (source, target) in enumerate(halo):
        moves.append(pltpu.make_async_copy(source, target, sems.at[place]))
    for move in moves:
        move.start()

    for place, gain in enumerate((one_in, two_in)):
        gains[place] = jnp.broadcast_to(0.5 * gain[...].reshape(1, channels), (width, channels)).T
    gain_one, gain_two = gains.at[0], gains.at[1]

    across = width // cells
    column = lax.broadcasted_iota(jnp.int32, (cells, width), 1)
    cell = lax.broadcasted_iota(jnp.int32, (cells, width), 0) * across
    expand = ((column >= cell) & (column < cell + across)).astype(jnp.float32).astype(jnp.bfloat16)
    lane = lax.broadcasted_iota(jnp.int32, (channels, width), 1)

    def spread(source):
        by_slot = [
            lax.dot_general(
                source[slot], expand, (((0,), (0,)), ((), ())), preferred_element_type=jnp.float32
            )
            for slot in range(2)
        ]
        middle = jnp.where(first_slot, by_slot[1], by_slot[0])
        return [by_slot[0], middle, middle, by_slot[1]]

    def norm(values, gain, scale):
        square = jnp.sum(values * values, axis=0, keepdims=True) * (1.0 / channels)
        inverse = lax.rsqrt(square + 1e-06)
        if scale is not None:
            inverse = inverse * scale
        half = values * inverse * gain[...]
        return half + half * jnp.tanh(half)

    def keep(frame, position, pixels, added, scale):
        total = (pixels.astype(jnp.float32) + added).astype(jnp.bfloat16)
        if frame in (1, 2) and 1 <= position <= 4:
            merged[frame - 1, position - 1] = total
        normed = norm(total.astype(jnp.float32), gain_one, scale)
        normed = normed.astype(jnp.bfloat16)
        before = jnp.where(lane == 0, jnp.zeros_like(normed), pltpu.roll(normed, 1, 1))
        after = jnp.where(lane == width - 1, jnp.zeros_like(normed), pltpu.roll(normed, width - 1, 1))
        half, side = ((1, 0), (0, 0), (0, 1), (1, 1))[frame]
        lanes = pl.ds(width * side, width)
        for place, part in enumerate((before, normed, after)):
            stack[half, position, pl.ds(place * channels, channels), lanes] = part

    here, further = spread(up_own), spread(up_next)
    held = (left.at[0], own.at[0], own.at[1], right.at[0])

    halves = ((1, 2), (0, 3))

    def first_norm(half, position):
        for frame in halves[half]:
            if position == 0:
                pixels = jnp.where(even, beyond[frame], pair[frame])
                added = jnp.where(even, further[frame], here[frame])
                keep(frame, 0, pixels, added, valid_above)
            elif position == 5:
                pixels = jnp.where(even, pair[frame], beyond[frame])
                added = jnp.where(even, here[frame], further[frame])
                keep(frame, 5, pixels, added, valid_below)
            else:
                keep(frame, position, held[frame][position - 1], here[frame], None)

    def convolve(half, row_out):
        window = stack[half, pl.ds(row_out, 3)].reshape(9 * channels, 2 * width)
        return jnp.dot(space[...], window, preferred_element_type=jnp.float32)

    def second_norm(half, row_out, spatial):
        for side in range(2):
            frame = halves[half][side]
            scale = (valid_before, None, None, valid_after)[frame]
            normed = norm(spatial[:, side * width : (side + 1) * width], gain_two, scale)
            second[row_out // 2, frame, :, pl.ds(width * (row_out % 2), width)] = normed.astype(
                jnp.bfloat16
            )

    for move in moves:
        move.wait()
    for position in (1, 2, 3):
        first_norm(0, position)
    order = ((0, 1), (0, 2), (0, 0), (0, 3), (1, 1), (1, 2), (1, 0), (1, 3))
    ahead = {
        (0, 1): ((0, 4), (0, 0)),
        (0, 2): ((0, 5), (1, 1)),
        (0, 0): ((1, 2),),
        (0, 3): ((1, 3),),
        (1, 1): ((1, 4), (1, 0)),
        (1, 2): ((1, 5),),
    }
    waiting = None
    for half, row_out in order:
        current = convolve(half, row_out)
        for other in ahead.get((half, row_out), ()):
            first_norm(*other)
        if waiting is not None:
            second_norm(*waiting)
        waiting = (half, row_out, current)
    second_norm(*waiting)

    for frame in range(2):
        for half in range(2):
            window = second[half, pl.ds(frame, 3)].reshape(3 * channels, 2 * width)
            temporal = jnp.dot(time[...], window, preferred_element_type=jnp.float32)
            for side in range(2):
                row_out = 2 * half + side
                sums = merged[frame, row_out].astype(jnp.float32)
                sums += temporal[:, side * width : (side + 1) * width]
                mixed[frame, pl.ds(row_out, channels, stride=4), :] = sums
        turned[frame] = mixed[frame].reshape(channels, 4, width).astype(jnp.bfloat16)
        leave = pltpu.make_async_copy(turned.at[frame], out.at[frame], out_sems.at[frame])
        leave.start()
        leaving.append(leave)
    for leave in leaving:
        leave.wait()


def fine_stage(own, left, right, pair, beyond, up_own, up_next, gain_one, gain_two, space, time):
    channels, width = own.shape[2:]
    bf16 = jnp.bfloat16
    copied = (left, right, pair, beyond)
    return pl.pallas_call(
        fine_kernel,
        out_shape=jax.ShapeDtypeStruct((2, channels, 4, width), bf16),
        in_specs=[VMEM] + [HBM] * 4 + [VMEM] * 6,
        out_specs=HBM,
        scratch_shapes=[pltpu.VMEM(array.shape, array.dtype) for array in copied]
        + [
            pltpu.VMEM((2, channels, width), jnp.float32),
            pltpu.VMEM((2, 6, 3 * channels, 2 * width), bf16),
            pltpu.VMEM((2, 4, channels, 2 * width), bf16),
            pltpu.VMEM((2, 4, channels, width), bf16),
            pltpu.VMEM((2, 4 * channels, width), jnp.float32),
            pltpu.VMEM((2, channels, 4, width), bf16),
            pltpu.SemaphoreType.DMA((len(copied),)),
            pltpu.SemaphoreType.DMA((2,)),
        ],
        compiler_params=limit(28),
        name="fine_stage",
    )(own, left, right, pair, beyond, up_own, up_next, gain_one, gain_two, space, time)


def local(fine, coarse, w_qkv, w_out, w_up, gain_one, conv_space, gain_two, conv_time):
    frames = lax.axis_size("frame")
    rows = lax.axis_size("row")
    cf, cells, c_dev = coarse.shape
    fine_c, width = fine.shape[1], fine.shape[3]
    tokens = cf * cells
    share = 8
    groups = [list(range(k, k + share)) for k in range(0, rows, share)]
    partner = [(i, i ^ 1) for i in range(rows)]
    across = [(i, i + 1) for i in range(1, rows - 1, 2)]
    across += [(b, a) for a, b in across]

    message = pack(coarse, w_up, share, frames)
    arrived = lax.all_to_all(message, "frame", 0, 0, tiled=True)

    rows_first = jnp.swapaxes(fine, 1, 2)
    left = lax.ppermute(rows_first[1:], "frame", [(i, i + 1) for i in range(frames - 1)])
    right = lax.ppermute(rows_first[:1], "frame", [(i + 1, i) for i in range(frames - 1)])
    space = jnp.transpose(conv_space, (3, 0, 1, 2)).reshape(fine_c, 9 * fine_c)
    time = jnp.transpose(conv_time, (2, 0, 1)).reshape(fine_c, 3 * fine_c)

    copies, whole = fold(arrived, w_out, tokens, share)
    folded = lax.all_to_all(copies, "row", 0, 0, tiled=True, axis_index_groups=groups)
    folded = folded.reshape(fine_c, w_out.shape[0])
    mine = attend(whole, jnp.swapaxes(w_qkv, 1, 2), coarse)
    other = lax.ppermute(mine, "row", partner)

    per = frames // cf
    wanted = []
    for f in range(frames):
        wanted.append(max(f - 1, 0) // per)
        wanted.append(min(f + 1, frames - 1) // per)
    outgoing = project(mine, other, folded, w_up, wanted).reshape(frames, 2, 2 * cells, fine_c)
    summed = lax.all_to_all(outgoing, "frame", 0, 0, tiled=True)

    to_pair, to_next = edge_rows(left, rows_first, right, (outgoing, space, time))
    from_pair = lax.ppermute(to_pair, "row", partner)
    from_next = lax.ppermute(to_next, "row", across)

    up_own = total(summed)
    up_next = lax.ppermute(up_own, "row", across)
    return fine_stage(
        rows_first, left, right, from_pair, from_next, up_own, up_next, gain_one, gain_two, space, time
    )


def solution(mesh):
    return jax.shard_map(
        local,
        mesh=mesh,
        in_specs=(
            P("frame", None, "row", None),
            P(None, "row", "frame"),
            P(None, None, "frame"),
            P("frame", None),
            P("frame", None),
            P(),
            P(),
            P(),
            P(),
        ),
        out_specs=P("frame", None, "row", None),
        check_vma=False,
    )
```

```python
import math

import jax
import jax.numpy as jnp
from jax import lax
from jax.experimental import pallas as pl
from jax.experimental.pallas import tpu as pltpu
from jax.sharding import PartitionSpec as P

HD = 80
VMEM = pl.BlockSpec(memory_space=pltpu.VMEM)
ANY = pl.BlockSpec(memory_space=pl.ANY)
HBM = pl.BlockSpec(memory_space=pltpu.HBM)
FREE = pl.CostEstimate(flops=0, bytes_accessed=0, transcendentals=0)


def limit(mib):
    return pltpu.CompilerParams(vmem_limit_bytes=mib * 2**20)


def pack(coarse, w_up, share, count):
    cf, cells, depth = coarse.shape
    columns = w_up.shape[1] // share

    def body(coarse_in, up_in, out_ref, coarse_ref, up_ref, sems):
        moves = [
            pltpu.make_async_copy(coarse_in, coarse_ref, sems.at[0]),
            pltpu.make_async_copy(up_in, up_ref, sems.at[1]),
        ]
        for move in moves:
            move.start()
        for move in moves:
            move.wait()
        first = lax.rem(lax.axis_index("row"), share) * columns
        shape = (columns, w_up.shape[1])
        wanted = lax.broadcasted_iota(jnp.int32, shape, 0) + first
        pick = (lax.broadcasted_iota(jnp.int32, shape, 1) == wanted).astype(jnp.float32)
        rows = lax.dot_general(
            pick.astype(jnp.bfloat16),
            up_ref[...],
            (((1,), (1,)), ((), ())),
            preferred_element_type=jnp.float32,
        ).astype(jnp.bfloat16)
        for place in range(count):
            for frame in range(cf):
                out_ref[place, pl.ds(frame * cells, cells)] = coarse_ref[frame]
            out_ref[place, pl.ds(cf * cells, columns)] = rows

    return pl.pallas_call(
        body,
        out_shape=jax.ShapeDtypeStruct((count, cf * cells + columns, depth), jnp.bfloat16),
        in_specs=[HBM] * 2,
        out_specs=VMEM,
        scratch_shapes=[
            pltpu.VMEM(coarse.shape, coarse.dtype),
            pltpu.VMEM(w_up.shape, w_up.dtype),
            pltpu.SemaphoreType.DMA((2,)),
        ],
        compiler_params=limit(56),
        cost_estimate=FREE,
        name="pack",
    )(coarse, w_up)


def fold(arrived, w_out, tokens, count):
    blocks, rows, depth = arrived.shape
    heads = w_out.shape[0]

    def body(arrived_ref, out_w_ref, out_ref, cells_ref, whole_ref):
        for block in range(blocks):
            whole_ref[:, pl.ds(block * depth, depth)] = arrived_ref[block]
        cells_ref[...] = whole_ref[pl.ds(0, tokens)]
        total = lax.dot_general(
            whole_ref[pl.ds(tokens, rows - tokens)],
            out_w_ref[...],
            (((1,), (1,)), ((), ())),
            preferred_element_type=jnp.float32,
        ).astype(jnp.bfloat16)
        for place in range(count):
            out_ref[place] = total

    return pl.pallas_call(
        body,
        out_shape=(
            jax.ShapeDtypeStruct((count, rows - tokens, heads), jnp.bfloat16),
            jax.ShapeDtypeStruct((tokens, blocks * depth), jnp.bfloat16),
        ),
        in_specs=[VMEM] * 2,
        out_specs=(VMEM, VMEM),
        scratch_shapes=[pltpu.VMEM((rows, blocks * depth), jnp.bfloat16)],
        compiler_params=limit(2),
        cost_estimate=FREE,
        name="fold",
    )(arrived, w_out)


def attend(whole, w_qkv_t, coarse):
    cf, cells, depth = coarse.shape

    def body(whole_ref, w_ref, coarse_ref, out_ref):
        projected = []
        for part in range(3):
            value = lax.dot_general(
                whole_ref[...],
                w_ref[part],
                (((1,), (1,)), ((), ())),
                preferred_element_type=jnp.float32,
            )
            value = value.astype(jnp.bfloat16).astype(jnp.float32)
            projected.append([value[cells * f : cells * (f + 1)] for f in range(cf)])
        query, keys, values = projected
        for f in range(cf):
            scores = [
                jnp.sum(query[f] * keys[g], axis=1, keepdims=True) * (1.0 / math.sqrt(HD))
                for g in range(cf)
            ]
            most = scores[0]
            for score in scores[1:]:
                most = jnp.maximum(most, score)
            weights = [jnp.exp(score - most) for score in scores]
            total = sum(weights[1:], weights[0])
            mixed = None
            for g in range(cf):
                share = (weights[g] / total).astype(jnp.bfloat16).astype(jnp.float32)
                term = share * values[g]
                mixed = term if mixed is None else mixed + term
            out_ref[0, f] = mixed.astype(jnp.bfloat16)
            out_ref[1, f] = coarse_ref[f]

    return pl.pallas_call(
        body,
        out_shape=jax.ShapeDtypeStruct((2, *coarse.shape), jnp.bfloat16),
        in_specs=[VMEM] * 3,
        out_specs=VMEM,
        compiler_params=limit(2),
        cost_estimate=pl.CostEstimate(flops=10000000000, bytes_accessed=0, transcendentals=0),
        name="attend",
    )(whole, w_qkv_t, coarse)


def project(mine, folded, w_up, wanted):
    cf, cells, width = mine.shape[1:]

    def body(mine_ref, folded_ref, up_ref, out_ref):
        attn = mine_ref[0].reshape(cf * cells, width)
        inputs = mine_ref[1].reshape(cf * cells, width)
        partial = lax.dot_general(
            attn, folded_ref[...], (((1,), (1,)), ((), ())), preferred_element_type=jnp.float32
        )
        partial += jnp.dot(inputs, up_ref[...], preferred_element_type=jnp.float32)
        for f in range(cf):
            block = partial[cells * f : cells * (f + 1)].astype(jnp.bfloat16)
            for place, source in enumerate(wanted):
                if source == f:
                    out_ref[place] = block

    return pl.pallas_call(
        body,
        out_shape=jax.ShapeDtypeStruct((len(wanted), cells, w_up.shape[1]), jnp.bfloat16),
        in_specs=[VMEM] * 3,
        out_specs=VMEM,
        compiler_params=limit(2),
        cost_estimate=FREE,
        name="project",
    )(mine, folded, w_up)


def edge_rows(left, own, right, earlier):
    rows, channels, width = own.shape[1:]

    def body(left_ref, own_ref, right_ref, *refs):
        pair_ref, next_ref, sems = refs[-3:]
        odd = lax.rem(lax.axis_index("row"), 2)
        frames = (left_ref.at[0], own_ref.at[0], own_ref.at[1], right_ref.at[0])
        moves = []
        for place, frame in enumerate(frames):
            for side, (out, row) in enumerate(((pair_ref, 1 - odd), (next_ref, odd))):
                moves.append(
                    pltpu.make_async_copy(
                        frame.at[row * (rows - 1)], out.at[place], sems.at[2 * place + side]
                    )
                )
        for move in moves:
            move.start()
        for move in moves:
            move.wait()

    shape = jax.ShapeDtypeStruct((4, channels, width), jnp.bfloat16)
    return pl.pallas_call(
        body,
        out_shape=(shape, shape),
        in_specs=[ANY] * (3 + len(earlier)),
        out_specs=(VMEM, VMEM),
        scratch_shapes=[pltpu.SemaphoreType.DMA((8,))],
        compiler_params=limit(2),
        cost_estimate=FREE,
        name="edge_rows",
    )(left, own, right, *earlier)


def total(summed):
    def body(summed_ref, out_ref):
        result = summed_ref[0].astype(jnp.float32)
        for source in range(1, summed.shape[0]):
            result += summed_ref[source].astype(jnp.float32)
        out_ref[...] = result.astype(jnp.bfloat16)

    return pl.pallas_call(
        body,
        out_shape=jax.ShapeDtypeStruct(summed.shape[1:], jnp.bfloat16),
        in_specs=[VMEM],
        out_specs=VMEM,
        compiler_params=limit(2),
        cost_estimate=pl.CostEstimate(flops=10000000000, bytes_accessed=0, transcendentals=0),
        name="total",
    )(summed)


def fine_kernel(
    own, left_in, right_in, pair_in, next_in, up_own, up_pair, up_near, up_far, one_in, two_in, space, time,
    out, left, right, pair, beyond, gains, stack, second, merged, mixed, turned, sems, out_sems,
):
    channels, width = own.shape[2:]
    cells = 2 * up_own.shape[1]
    row, frame_index = lax.axis_index("row"), lax.axis_index("frame")
    last_row, last_frame = lax.axis_size("row") - 1, lax.axis_size("frame") - 1
    even = lax.rem(row, 2) == 0
    first_slot = lax.rem(frame_index, 4) == 0
    valid_above = (row > 0).astype(jnp.float32)
    valid_below = (row < last_row).astype(jnp.float32)
    valid_before = (frame_index > 0).astype(jnp.float32)
    valid_after = (frame_index < last_frame).astype(jnp.float32)

    moves, leaving = [], []
    halo = ((left_in, left), (right_in, right), (pair_in, pair), (next_in, beyond))
    for place, (source, target) in enumerate(halo):
        moves.append(pltpu.make_async_copy(source, target, sems.at[place]))
    for move in moves:
        move.start()

    for place, gain in enumerate((one_in, two_in)):
        gains[place] = jnp.broadcast_to(0.5 * gain[...].reshape(1, channels), (width, channels)).T
    gain_one, gain_two = gains.at[0], gains.at[1]

    def columns_of(odd):
        cell = lax.broadcasted_iota(jnp.int32, (cells, width), 0) + odd * (cells // 2)
        cell = jnp.where(cell >= cells, cell - cells, cell) * (width // cells)
        column = lax.broadcasted_iota(jnp.int32, (cells, width), 1)
        inside = (column >= cell) & (column < cell + width // cells)
        return inside.astype(jnp.float32).astype(jnp.bfloat16)

    lane = lax.broadcasted_iota(jnp.int32, (channels, width), 1)

    def spread(first, then, expand):
        by_slot = []
        for slot in range(2):
            both = jnp.concatenate(
                [first[slot].astype(jnp.float32), then[slot].astype(jnp.float32)], axis=0
            )
            by_slot.append(
                lax.dot_general(
                    both.astype(jnp.bfloat16),
                    expand,
                    (((0,), (0,)), ((), ())),
                    preferred_element_type=jnp.float32,
                )
            )
        middle = jnp.where(first_slot, by_slot[1], by_slot[0])
        return [by_slot[0], middle, middle, by_slot[1]]

    def norm(values, gain, scale):
        square = jnp.sum(values * values, axis=0, keepdims=True) * (1.0 / channels)
        inverse = lax.rsqrt(square + 1e-06)
        if scale is not None:
            inverse = inverse * scale
        half = values * inverse * gain[...]
        return half + half * jnp.tanh(half)

    def keep(frame, position, pixels, added, scale):
        total = (pixels.astype(jnp.float32) + added).astype(jnp.bfloat16)
        if frame in (1, 2) and 1 <= position <= 4:
            merged[frame - 1, position - 1] = total
        normed = norm(total.astype(jnp.float32), gain_one, scale)
        normed = normed.astype(jnp.bfloat16)
        before = jnp.where(lane == 0, jnp.zeros_like(normed), pltpu.roll(normed, 1, 1))
        after = jnp.where(lane == width - 1, jnp.zeros_like(normed), pltpu.roll(normed, width - 1, 1))
        half, side = ((1, 0), (0, 0), (0, 1), (1, 1))[frame]
        lanes = pl.ds(width * side, width)
        for place, part in enumerate((before, normed, after)):
            stack[half, position, pl.ds(place * channels, channels), lanes] = part

    odd = lax.rem(row, 2)
    here = spread(up_own, up_pair, columns_of(odd))
    further = spread(up_near, up_far, columns_of(1 - odd))
    held = (left.at[0], own.at[0], own.at[1], right.at[0])

    halves = ((1, 2), (0, 3))

    def first_norm(half, position):
        for frame in halves[half]:
            if position == 0:
                pixels = jnp.where(even, beyond[frame], pair[frame])
                added = jnp.where(even, further[frame], here[frame])
                keep(frame, 0, pixels, added, valid_above)
            elif position == 5:
                pixels = jnp.where(even, pair[frame], beyond[frame])
                added = jnp.where(even, here[frame], further[frame])
                keep(frame, 5, pixels, added, valid_below)
            else:
                keep(frame, position, held[frame][position - 1], here[frame], None)

    def convolve(half, row_out):
        window = stack[half, pl.ds(row_out, 3)].reshape(9 * channels, 2 * width)
        return jnp.dot(space[...], window, preferred_element_type=jnp.float32)

    def second_norm(half, row_out, spatial):
        for side in range(2):
            frame = halves[half][side]
            scale = (valid_before, None, None, valid_after)[frame]
            normed = norm(spatial[:, side * width : (side + 1) * width], gain_two, scale)
            second[row_out // 2, frame, :, pl.ds(width * (row_out % 2), width)] = normed.astype(
                jnp.bfloat16
            )

    for move in moves:
        move.wait()
    for position in (1, 2, 3):
        first_norm(0, position)
    order = ((0, 1), (0, 2), (0, 0), (0, 3), (1, 1), (1, 2), (1, 0), (1, 3))
    ahead = {
        (0, 1): ((0, 4), (0, 0)),
        (0, 2): ((0, 5), (1, 1)),
        (0, 0): ((1, 2),),
        (0, 3): ((1, 3),),
        (1, 1): ((1, 4), (1, 0)),
        (1, 2): ((1, 5),),
    }
    waiting = None
    for half, row_out in order:
        current = convolve(half, row_out)
        for other in ahead.get((half, row_out), ()):
            first_norm(*other)
        if waiting is not None:
            second_norm(*waiting)
        waiting = (half, row_out, current)
    second_norm(*waiting)

    for frame in range(2):
        for half in range(2):
            window = second[half, pl.ds(frame, 3)].reshape(3 * channels, 2 * width)
            temporal = jnp.dot(time[...], window, preferred_element_type=jnp.float32)
            for side in range(2):
                row_out = 2 * half + side
                sums = merged[frame, row_out].astype(jnp.float32)
                sums += temporal[:, side * width : (side + 1) * width]
                mixed[frame, pl.ds(row_out, channels, stride=4), :] = sums
        turned[frame] = mixed[frame].reshape(channels, 4, width).astype(jnp.bfloat16)
        leave = pltpu.make_async_copy(turned.at[frame], out.at[frame], out_sems.at[frame])
        leave.start()
        leaving.append(leave)
    for leave in leaving:
        leave.wait()


def fine_stage(own, left, right, pair, beyond, up_own, up_pair, up_near, up_far, gain_one, gain_two, space, time):
    channels, width = own.shape[2:]
    bf16 = jnp.bfloat16
    copied = (left, right, pair, beyond)
    return pl.pallas_call(
        fine_kernel,
        out_shape=jax.ShapeDtypeStruct((2, channels, 4, width), bf16),
        in_specs=[VMEM] + [HBM] * 4 + [VMEM] * 8,
        out_specs=HBM,
        scratch_shapes=[pltpu.VMEM(array.shape, array.dtype) for array in copied]
        + [
            pltpu.VMEM((2, channels, width), jnp.float32),
            pltpu.VMEM((2, 6, 3 * channels, 2 * width), bf16),
            pltpu.VMEM((2, 4, channels, 2 * width), bf16),
            pltpu.VMEM((2, 4, channels, width), bf16),
            pltpu.VMEM((2, 4 * channels, width), jnp.float32),
            pltpu.VMEM((2, channels, 4, width), bf16),
            pltpu.SemaphoreType.DMA((len(copied),)),
            pltpu.SemaphoreType.DMA((2,)),
        ],
        compiler_params=limit(28),
        name="fine_stage",
    )(own, left, right, pair, beyond, up_own, up_pair, up_near, up_far, gain_one, gain_two, space, time)


def local(fine, coarse, w_qkv, w_out, w_up, gain_one, conv_space, gain_two, conv_time):
    frames = lax.axis_size("frame")
    rows = lax.axis_size("row")
    cf, cells, c_dev = coarse.shape
    fine_c, width = fine.shape[1], fine.shape[3]
    tokens = cf * cells
    share = 8
    groups = [list(range(k, k + share)) for k in range(0, rows, share)]
    partner = [(i, i ^ 1) for i in range(rows)]
    across = [(i, i + 1) for i in range(1, rows - 1, 2)]
    across += [(b, a) for a, b in across]
    beyond = [(i, i + 2) for i in range(0, rows - 2, 2)] + [(i + 2, i) for i in range(1, rows - 2, 2)]

    message = pack(coarse, w_up, share, frames)
    arrived = lax.all_to_all(message, "frame", 0, 0, tiled=True)

    rows_first = jnp.swapaxes(fine, 1, 2)
    left = lax.ppermute(rows_first[1:], "frame", [(i, i + 1) for i in range(frames - 1)])
    right = lax.ppermute(rows_first[:1], "frame", [(i + 1, i) for i in range(frames - 1)])

    copies, whole = fold(arrived, w_out, tokens, share)
    folded = lax.all_to_all(copies, "row", 0, 0, tiled=True, axis_index_groups=groups)
    folded = folded.reshape(fine_c, w_out.shape[0])
    mine = attend(whole, jnp.swapaxes(w_qkv, 1, 2), coarse)

    per = frames // cf
    wanted = []
    for f in range(frames):
        wanted.append(max(f - 1, 0) // per)
        wanted.append(min(f + 1, frames - 1) // per)
    outgoing = project(mine, folded, w_up, wanted).reshape(frames, 2, cells, fine_c)
    summed = lax.all_to_all(outgoing, "frame", 0, 0, tiled=True)

    conv_space, conv_time, _ = lax.optimization_barrier((conv_space, conv_time, outgoing))
    space = jnp.transpose(conv_space, (3, 0, 1, 2)).reshape(fine_c, 9 * fine_c)
    time = jnp.transpose(conv_time, (2, 0, 1)).reshape(fine_c, 3 * fine_c)
    to_pair, to_next = edge_rows(left, rows_first, right, (outgoing, space, time))
    from_pair = lax.ppermute(to_pair, "row", partner)
    from_next = lax.ppermute(to_next, "row", across)

    up_own = total(summed)
    up_pair = lax.ppermute(up_own, "row", partner)
    up_near = lax.ppermute(up_own, "row", across)
    up_far = lax.ppermute(up_own, "row", beyond)
    return fine_stage(
        rows_first, left, right, from_pair, from_next, up_own, up_pair, up_near, up_far, gain_one, gain_two, space, time
    )


def solution(mesh):
    return jax.shard_map(
        local,
        mesh=mesh,
        in_specs=(
            P("frame", None, "row", None),
            P(None, "row", "frame"),
            P(None, None, "frame"),
            P("frame", None),
            P("frame", None),
            P(),
            P(),
            P(),
            P(),
        ),
        out_specs=P("frame", None, "row", None),
        check_vma=False,
    )
```

```python
import math

import jax
import jax.numpy as jnp
from jax import lax
from jax.experimental import pallas as pl
from jax.experimental.pallas import tpu as pltpu
from jax.sharding import PartitionSpec as P

HD = 80
VMEM = pl.BlockSpec(memory_space=pltpu.VMEM)
ANY = pl.BlockSpec(memory_space=pl.ANY)
HBM = pl.BlockSpec(memory_space=pltpu.HBM)
FREE = pl.CostEstimate(flops=0, bytes_accessed=0, transcendentals=0)


def limit(mib):
    return pltpu.CompilerParams(vmem_limit_bytes=mib * 2**20)


def pack(coarse, w_up, share, count):
    cf, cells, depth = coarse.shape
    columns = w_up.shape[1] // share

    def body(coarse_in, up_in, out_ref, coarse_ref, up_ref, sems):
        moves = [
            pltpu.make_async_copy(coarse_in, coarse_ref, sems.at[0]),
            pltpu.make_async_copy(up_in, up_ref, sems.at[1]),
        ]
        for move in moves:
            move.start()
        for move in moves:
            move.wait()
        first = lax.rem(lax.axis_index("row"), share) * columns
        shape = (columns, w_up.shape[1])
        wanted = lax.broadcasted_iota(jnp.int32, shape, 0) + first
        pick = (lax.broadcasted_iota(jnp.int32, shape, 1) == wanted).astype(jnp.float32)
        rows = lax.dot_general(
            pick.astype(jnp.bfloat16),
            up_ref[...],
            (((1,), (1,)), ((), ())),
            preferred_element_type=jnp.float32,
        ).astype(jnp.bfloat16)
        for place in range(count):
            for frame in range(cf):
                out_ref[place, pl.ds(frame * cells, cells)] = coarse_ref[frame]
            out_ref[place, pl.ds(cf * cells, columns)] = rows

    return pl.pallas_call(
        body,
        out_shape=jax.ShapeDtypeStruct((count, cf * cells + columns, depth), jnp.bfloat16),
        in_specs=[HBM] * 2,
        out_specs=VMEM,
        scratch_shapes=[
            pltpu.VMEM(coarse.shape, coarse.dtype),
            pltpu.VMEM(w_up.shape, w_up.dtype),
            pltpu.SemaphoreType.DMA((2,)),
        ],
        compiler_params=limit(56),
        cost_estimate=FREE,
        name="pack",
    )(coarse, w_up)


def fold(arrived, w_out, tokens, count):
    blocks, rows, depth = arrived.shape
    heads = w_out.shape[0]

    def body(arrived_ref, out_w_ref, out_ref, cells_ref, whole_ref):
        for block in range(blocks):
            whole_ref[:, pl.ds(block * depth, depth)] = arrived_ref[block]
        cells_ref[...] = whole_ref[pl.ds(0, tokens)]
        total = lax.dot_general(
            whole_ref[pl.ds(tokens, rows - tokens)],
            out_w_ref[...],
            (((1,), (1,)), ((), ())),
            preferred_element_type=jnp.float32,
        ).astype(jnp.bfloat16)
        for place in range(count):
            out_ref[place] = total

    return pl.pallas_call(
        body,
        out_shape=(
            jax.ShapeDtypeStruct((count, rows - tokens, heads), jnp.bfloat16),
            jax.ShapeDtypeStruct((tokens, blocks * depth), jnp.bfloat16),
        ),
        in_specs=[VMEM] * 2,
        out_specs=(VMEM, VMEM),
        scratch_shapes=[pltpu.VMEM((rows, blocks * depth), jnp.bfloat16)],
        compiler_params=limit(2),
        cost_estimate=FREE,
        name="fold",
    )(arrived, w_out)


def attend(whole, w_qkv_t, coarse):
    cf, cells, depth = coarse.shape

    def body(whole_ref, w_ref, coarse_ref, out_ref):
        projected = []
        for part in range(3):
            value = lax.dot_general(
                whole_ref[...],
                w_ref[part],
                (((1,), (1,)), ((), ())),
                preferred_element_type=jnp.float32,
            )
            value = value.astype(jnp.bfloat16).astype(jnp.float32)
            projected.append([value[cells * f : cells * (f + 1)] for f in range(cf)])
        query, keys, values = projected
        for f in range(cf):
            scores = [
                jnp.sum(query[f] * keys[g], axis=1, keepdims=True) * (1.0 / math.sqrt(HD))
                for g in range(cf)
            ]
            most = scores[0]
            for score in scores[1:]:
                most = jnp.maximum(most, score)
            weights = [jnp.exp(score - most) for score in scores]
            total = sum(weights[1:], weights[0])
            mixed = None
            for g in range(cf):
                share = (weights[g] / total).astype(jnp.bfloat16).astype(jnp.float32)
                term = share * values[g]
                mixed = term if mixed is None else mixed + term
            out_ref[0, f] = mixed.astype(jnp.bfloat16)
            out_ref[1, f] = coarse_ref[f]

    return pl.pallas_call(
        body,
        out_shape=jax.ShapeDtypeStruct((2, *coarse.shape), jnp.bfloat16),
        in_specs=[VMEM] * 3,
        out_specs=VMEM,
        compiler_params=limit(2),
        cost_estimate=pl.CostEstimate(flops=10000000000, bytes_accessed=0, transcendentals=0),
        name="attend",
    )(whole, w_qkv_t, coarse)


def project(mine, folded, w_up, earlier, wanted):
    cf, cells, width = mine.shape[1:]

    def body(mine_ref, folded_ref, up_ref, _, out_ref):
        attn = mine_ref[0].reshape(cf * cells, width)
        inputs = mine_ref[1].reshape(cf * cells, width)
        partial = lax.dot_general(
            attn, folded_ref[...], (((1,), (1,)), ((), ())), preferred_element_type=jnp.float32
        )
        partial += jnp.dot(inputs, up_ref[...], preferred_element_type=jnp.float32)
        for f in range(cf):
            block = partial[cells * f : cells * (f + 1)].astype(jnp.bfloat16)
            for place, source in enumerate(wanted):
                if source == f:
                    out_ref[place] = block

    return pl.pallas_call(
        body,
        out_shape=jax.ShapeDtypeStruct((len(wanted), cells, w_up.shape[1]), jnp.bfloat16),
        in_specs=[VMEM] * 3 + [ANY],
        out_specs=VMEM,
        compiler_params=limit(2),
        cost_estimate=FREE,
        name="project",
    )(mine, folded, w_up, earlier)


def edge_rows(left, one, two, right, earlier):
    rows, channels, width = one.shape[1:]

    def body(left_ref, one_ref, two_ref, right_ref, *refs):
        pair_ref, next_ref, sems = refs[-3:]
        odd = lax.rem(lax.axis_index("row"), 2)
        frames = (left_ref.at[0], one_ref.at[0], two_ref.at[0], right_ref.at[0])
        moves = []
        for place, frame in enumerate(frames):
            for side, (out, row) in enumerate(((pair_ref, 1 - odd), (next_ref, odd))):
                moves.append(
                    pltpu.make_async_copy(
                        frame.at[row * (rows - 1)], out.at[place], sems.at[2 * place + side]
                    )
                )
        for move in moves:
            move.start()
        for move in moves:
            move.wait()

    shape = jax.ShapeDtypeStruct((4, channels, width), jnp.bfloat16)
    return pl.pallas_call(
        body,
        out_shape=(shape, shape),
        in_specs=[ANY] * (4 + len(earlier)),
        out_specs=(VMEM, VMEM),
        scratch_shapes=[pltpu.SemaphoreType.DMA((8,))],
        compiler_params=limit(2),
        cost_estimate=FREE,
        name="edge_rows",
    )(left, one, two, right, *earlier)


def total(summed):
    def body(summed_ref, out_ref):
        result = summed_ref[0].astype(jnp.float32)
        for source in range(1, summed.shape[0]):
            result += summed_ref[source].astype(jnp.float32)
        out_ref[...] = result.astype(jnp.bfloat16)

    return pl.pallas_call(
        body,
        out_shape=jax.ShapeDtypeStruct(summed.shape[1:], jnp.bfloat16),
        in_specs=[VMEM],
        out_specs=VMEM,
        compiler_params=limit(2),
        cost_estimate=pl.CostEstimate(flops=10000000000, bytes_accessed=0, transcendentals=0),
        name="total",
    )(summed)


def fine_kernel(
    one, two, left_in, right_in, pair_in, next_in, up_own, up_pair, up_near, up_far, one_in, two_in, space, time,
    out, left, right, pair, beyond, gains, stack, second, merged, mixed, turned, sems, out_sems,
):
    channels, width = one.shape[2:]
    cells = 2 * up_own.shape[1]
    row, frame_index = lax.axis_index("row"), lax.axis_index("frame")
    last_row, last_frame = lax.axis_size("row") - 1, lax.axis_size("frame") - 1
    even = lax.rem(row, 2) == 0
    first_slot = lax.rem(frame_index, 4) == 0
    valid_above = (row > 0).astype(jnp.float32)
    valid_below = (row < last_row).astype(jnp.float32)
    valid_before = (frame_index > 0).astype(jnp.float32)
    valid_after = (frame_index < last_frame).astype(jnp.float32)

    moves, leaving = [], []
    halo = ((left_in, left), (right_in, right), (pair_in, pair), (next_in, beyond))
    for place, (source, target) in enumerate(halo):
        moves.append(pltpu.make_async_copy(source, target, sems.at[place]))
    for move in moves:
        move.start()

    for place, gain in enumerate((one_in, two_in)):
        gains[place] = jnp.broadcast_to(0.5 * gain[...].reshape(1, channels), (width, channels)).T
    gain_one, gain_two = gains.at[0], gains.at[1]

    def columns_of(odd):
        cell = lax.broadcasted_iota(jnp.int32, (cells, width), 0) + odd * (cells // 2)
        cell = jnp.where(cell >= cells, cell - cells, cell) * (width // cells)
        column = lax.broadcasted_iota(jnp.int32, (cells, width), 1)
        inside = (column >= cell) & (column < cell + width // cells)
        return inside.astype(jnp.float32).astype(jnp.bfloat16)

    lane = lax.broadcasted_iota(jnp.int32, (channels, width), 1)

    def spread(first, then, expand):
        by_slot = []
        for slot in range(2):
            both = jnp.concatenate(
                [first[slot].astype(jnp.float32), then[slot].astype(jnp.float32)], axis=0
            )
            by_slot.append(
                lax.dot_general(
                    both.astype(jnp.bfloat16),
                    expand,
                    (((0,), (0,)), ((), ())),
                    preferred_element_type=jnp.float32,
                )
            )
        middle = jnp.where(first_slot, by_slot[1], by_slot[0])
        return [by_slot[0], middle, middle, by_slot[1]]

    def norm(values, gain, scale):
        square = jnp.sum(values * values, axis=0, keepdims=True) * (1.0 / channels)
        inverse = lax.rsqrt(square + 1e-06)
        if scale is not None:
            inverse = inverse * scale
        half = values * inverse * gain[...]
        return half + half * jnp.tanh(half)

    def keep(frame, position, pixels, added, scale):
        total = (pixels.astype(jnp.float32) + added).astype(jnp.bfloat16)
        if frame in (1, 2) and 1 <= position <= 4:
            merged[frame - 1, position - 1] = total
        normed = norm(total.astype(jnp.float32), gain_one, scale)
        normed = normed.astype(jnp.bfloat16)
        before = jnp.where(lane == 0, jnp.zeros_like(normed), pltpu.roll(normed, 1, 1))
        after = jnp.where(lane == width - 1, jnp.zeros_like(normed), pltpu.roll(normed, width - 1, 1))
        half, side = ((1, 0), (0, 0), (0, 1), (1, 1))[frame]
        lanes = pl.ds(width * side, width)
        for place, part in enumerate((before, normed, after)):
            stack[half, position, pl.ds(place * channels, channels), lanes] = part

    odd = lax.rem(row, 2)
    here = spread(up_own, up_pair, columns_of(odd))
    further = spread(up_near, up_far, columns_of(1 - odd))
    held = (left.at[0], one.at[0], two.at[0], right.at[0])

    halves = ((1, 2), (0, 3))

    def first_norm(half, position):
        for frame in halves[half]:
            if position == 0:
                pixels = jnp.where(even, beyond[frame], pair[frame])
                added = jnp.where(even, further[frame], here[frame])
                keep(frame, 0, pixels, added, valid_above)
            elif position == 5:
                pixels = jnp.where(even, pair[frame], beyond[frame])
                added = jnp.where(even, here[frame], further[frame])
                keep(frame, 5, pixels, added, valid_below)
            else:
                keep(frame, position, held[frame][position - 1], here[frame], None)

    def convolve(half, row_out):
        window = stack[half, pl.ds(row_out, 3)].reshape(9 * channels, 2 * width)
        return jnp.dot(space[...], window, preferred_element_type=jnp.float32)

    def second_norm(half, row_out, spatial):
        for side in range(2):
            frame = halves[half][side]
            scale = (valid_before, None, None, valid_after)[frame]
            normed = norm(spatial[:, side * width : (side + 1) * width], gain_two, scale)
            second[row_out // 2, frame, :, pl.ds(width * (row_out % 2), width)] = normed.astype(
                jnp.bfloat16
            )

    for move in moves:
        move.wait()
    for position in (1, 2, 3):
        first_norm(0, position)
    order = ((0, 1), (0, 2), (0, 0), (0, 3), (1, 1), (1, 2), (1, 0), (1, 3))
    ahead = {
        (0, 1): ((0, 4), (0, 0)),
        (0, 2): ((0, 5), (1, 1)),
        (0, 0): ((1, 2),),
        (0, 3): ((1, 3),),
        (1, 1): ((1, 4), (1, 0)),
        (1, 2): ((1, 5),),
    }
    waiting = None
    for half, row_out in order:
        current = convolve(half, row_out)
        for other in ahead.get((half, row_out), ()):
            first_norm(*other)
        if waiting is not None:
            second_norm(*waiting)
        waiting = (half, row_out, current)
    second_norm(*waiting)

    for frame in range(2):
        for half in range(2):
            window = second[half, pl.ds(frame, 3)].reshape(3 * channels, 2 * width)
            temporal = jnp.dot(time[...], window, preferred_element_type=jnp.float32)
            for side in range(2):
                row_out = 2 * half + side
                sums = merged[frame, row_out].astype(jnp.float32)
                sums += temporal[:, side * width : (side + 1) * width]
                mixed[frame, pl.ds(row_out, channels, stride=4), :] = sums
        turned[frame] = mixed[frame].reshape(channels, 4, width).astype(jnp.bfloat16)
        leave = pltpu.make_async_copy(turned.at[frame], out.at[frame], out_sems.at[frame])
        leave.start()
        leaving.append(leave)
    for leave in leaving:
        leave.wait()


def fine_stage(one, two, left, right, pair, beyond, up_own, up_pair, up_near, up_far, gain_one, gain_two, space, time):
    channels, width = one.shape[2:]
    bf16 = jnp.bfloat16
    copied = (left, right, pair, beyond)
    return pl.pallas_call(
        fine_kernel,
        out_shape=jax.ShapeDtypeStruct((2, channels, 4, width), bf16),
        in_specs=[VMEM] * 2 + [HBM] * 4 + [VMEM] * 8,
        out_specs=HBM,
        scratch_shapes=[pltpu.VMEM(array.shape, array.dtype) for array in copied]
        + [
            pltpu.VMEM((2, channels, width), jnp.float32),
            pltpu.VMEM((2, 6, 3 * channels, 2 * width), bf16),
            pltpu.VMEM((2, 4, channels, 2 * width), bf16),
            pltpu.VMEM((2, 4, channels, width), bf16),
            pltpu.VMEM((2, 4 * channels, width), jnp.float32),
            pltpu.VMEM((2, channels, 4, width), bf16),
            pltpu.SemaphoreType.DMA((len(copied),)),
            pltpu.SemaphoreType.DMA((2,)),
        ],
        compiler_params=limit(28),
        name="fine_stage",
    )(one, two, left, right, pair, beyond, up_own, up_pair, up_near, up_far, gain_one, gain_two, space, time)


def local(fine, coarse, w_qkv, w_out, w_up, gain_one, conv_space, gain_two, conv_time):
    frames = lax.axis_size("frame")
    rows = lax.axis_size("row")
    cf, cells, c_dev = coarse.shape
    fine_c, width = fine.shape[1], fine.shape[3]
    tokens = cf * cells
    share = 8
    groups = [list(range(k, k + share)) for k in range(0, rows, share)]
    partner = [(i, i ^ 1) for i in range(rows)]
    across = [(i, i + 1) for i in range(1, rows - 1, 2)]
    across += [(b, a) for a, b in across]
    beyond = [(i, i + 2) for i in range(0, rows - 2, 2)] + [(i + 2, i) for i in range(1, rows - 2, 2)]

    message = pack(coarse, w_up, share, frames)
    arrived = lax.all_to_all(message, "frame", 0, 0, tiled=True)

    first, second = jnp.swapaxes(fine[:1], 1, 2), jnp.swapaxes(fine[1:], 1, 2)
    left = lax.ppermute(second, "frame", [(i, i + 1) for i in range(frames - 1)])
    right = lax.ppermute(first, "frame", [(i + 1, i) for i in range(frames - 1)])

    copies, whole = fold(arrived, w_out, tokens, share)
    folded = lax.all_to_all(copies, "row", 0, 0, tiled=True, axis_index_groups=groups)
    folded = folded.reshape(fine_c, w_out.shape[0])
    conv_space, _ = lax.optimization_barrier((conv_space, copies))
    space = jnp.transpose(conv_space, (3, 0, 1, 2)).reshape(fine_c, 9 * fine_c)
    mine = attend(whole, jnp.swapaxes(w_qkv, 1, 2), coarse)

    per = frames // cf
    wanted = []
    for f in range(frames):
        wanted.append(max(f - 1, 0) // per)
        wanted.append(min(f + 1, frames - 1) // per)
    outgoing = project(mine, folded, w_up, space, wanted).reshape(frames, 2, cells, fine_c)
    summed = lax.all_to_all(outgoing, "frame", 0, 0, tiled=True)

    conv_time, _ = lax.optimization_barrier((conv_time, outgoing))
    time = jnp.transpose(conv_time, (2, 0, 1)).reshape(fine_c, 3 * fine_c)
    to_pair, to_next = edge_rows(left, first, second, right, (outgoing, time))
    from_pair = lax.ppermute(to_pair, "row", partner)
    from_next = lax.ppermute(to_next, "row", across)

    up_own = total(summed)
    up_pair = lax.ppermute(up_own, "row", partner)
    up_near = lax.ppermute(up_own, "row", across)
    up_far = lax.ppermute(up_own, "row", beyond)
    return fine_stage(
        first, second, left, right, from_pair, from_next, up_own, up_pair, up_near, up_far, gain_one, gain_two, space, time
    )


def solution(mesh):
    return jax.shard_map(
        local,
        mesh=mesh,
        in_specs=(
            P("frame", None, "row", None),
            P(None, "row", "frame"),
            P(None, None, "frame"),
            P("frame", None),
            P("frame", None),
            P(),
            P(),
            P(),
            P(),
        ),
        out_specs=P("frame", None, "row", None),
        check_vma=False,
    )
```

```python
import math

import jax
import jax.numpy as jnp
from jax import lax
from jax.experimental import pallas as pl
from jax.experimental.pallas import tpu as pltpu
from jax.sharding import PartitionSpec as P

HD = 80
VMEM = pl.BlockSpec(memory_space=pltpu.VMEM)
ANY = pl.BlockSpec(memory_space=pl.ANY)
HBM = pl.BlockSpec(memory_space=pltpu.HBM)
FREE = pl.CostEstimate(flops=0, bytes_accessed=0, transcendentals=0)


def limit(mib):
    return pltpu.CompilerParams(vmem_limit_bytes=mib * 2**20)


def pack(coarse, w_up, share, count):
    cf, cells, depth = coarse.shape
    columns = w_up.shape[1] // share

    def body(coarse_in, up_in, out_ref, coarse_ref, up_ref, sems):
        moves = [
            pltpu.make_async_copy(coarse_in, coarse_ref, sems.at[0]),
            pltpu.make_async_copy(up_in, up_ref, sems.at[1]),
        ]
        for move in moves:
            move.start()
        for move in moves:
            move.wait()
        first = lax.rem(lax.axis_index("row"), share) * columns
        shape = (columns, w_up.shape[1])
        wanted = lax.broadcasted_iota(jnp.int32, shape, 0) + first
        pick = (lax.broadcasted_iota(jnp.int32, shape, 1) == wanted).astype(jnp.float32)
        rows = lax.dot_general(
            pick.astype(jnp.bfloat16),
            up_ref[...],
            (((1,), (1,)), ((), ())),
            preferred_element_type=jnp.float32,
        ).astype(jnp.bfloat16)
        for place in range(count):
            for frame in range(cf):
                out_ref[place, pl.ds(frame * cells, cells)] = coarse_ref[frame]
            out_ref[place, pl.ds(cf * cells, columns)] = rows

    return pl.pallas_call(
        body,
        out_shape=jax.ShapeDtypeStruct((count, cf * cells + columns, depth), jnp.bfloat16),
        in_specs=[HBM] * 2,
        out_specs=VMEM,
        scratch_shapes=[
            pltpu.VMEM(coarse.shape, coarse.dtype),
            pltpu.VMEM(w_up.shape, w_up.dtype),
            pltpu.SemaphoreType.DMA((2,)),
        ],
        compiler_params=limit(56),
        cost_estimate=FREE,
        name="pack",
    )(coarse, w_up)


def fold(arrived, w_out, tokens, count):
    blocks, rows, depth = arrived.shape
    heads = w_out.shape[0]

    def body(arrived_ref, out_w_ref, out_ref, cells_ref, whole_ref):
        for block in range(blocks):
            whole_ref[:, pl.ds(block * depth, depth)] = arrived_ref[block]
        cells_ref[...] = whole_ref[pl.ds(0, tokens)]
        total = lax.dot_general(
            whole_ref[pl.ds(tokens, rows - tokens)],
            out_w_ref[...],
            (((1,), (1,)), ((), ())),
            preferred_element_type=jnp.float32,
        ).astype(jnp.bfloat16)
        for place in range(count):
            out_ref[place] = total

    return pl.pallas_call(
        body,
        out_shape=(
            jax.ShapeDtypeStruct((count, rows - tokens, heads), jnp.bfloat16),
            jax.ShapeDtypeStruct((tokens, blocks * depth), jnp.bfloat16),
        ),
        in_specs=[VMEM] * 2,
        out_specs=(VMEM, VMEM),
        scratch_shapes=[pltpu.VMEM((rows, blocks * depth), jnp.bfloat16)],
        compiler_params=limit(2),
        cost_estimate=FREE,
        name="fold",
    )(arrived, w_out)


def attend(whole, w_qkv_t, coarse):
    cf, cells, depth = coarse.shape

    def body(whole_ref, w_ref, coarse_ref, out_ref):
        projected = []
        for part in range(3):
            value = lax.dot_general(
                whole_ref[...],
                w_ref[part],
                (((1,), (1,)), ((), ())),
                preferred_element_type=jnp.float32,
            )
            value = value.astype(jnp.bfloat16).astype(jnp.float32)
            projected.append([value[cells * f : cells * (f + 1)] for f in range(cf)])
        query, keys, values = projected
        for f in range(cf):
            scores = [
                jnp.sum(query[f] * keys[g], axis=1, keepdims=True) * (1.0 / math.sqrt(HD))
                for g in range(cf)
            ]
            most = scores[0]
            for score in scores[1:]:
                most = jnp.maximum(most, score)
            weights = [jnp.exp(score - most) for score in scores]
            total = sum(weights[1:], weights[0])
            mixed = None
            for g in range(cf):
                share = (weights[g] / total).astype(jnp.bfloat16).astype(jnp.float32)
                term = share * values[g]
                mixed = term if mixed is None else mixed + term
            out_ref[0, f] = mixed.astype(jnp.bfloat16)
            out_ref[1, f] = coarse_ref[f]

    return pl.pallas_call(
        body,
        out_shape=jax.ShapeDtypeStruct((2, *coarse.shape), jnp.bfloat16),
        in_specs=[VMEM] * 3,
        out_specs=VMEM,
        compiler_params=limit(2),
        cost_estimate=pl.CostEstimate(flops=10000000000, bytes_accessed=0, transcendentals=0),
        name="attend",
    )(whole, w_qkv_t, coarse)


def project(mine, folded, w_up, earlier, wanted):
    cf, cells, width = mine.shape[1:]

    def body(mine_ref, folded_ref, up_ref, _, out_ref):
        attn = mine_ref[0].reshape(cf * cells, width)
        inputs = mine_ref[1].reshape(cf * cells, width)
        partial = lax.dot_general(
            attn, folded_ref[...], (((1,), (1,)), ((), ())), preferred_element_type=jnp.float32
        )
        partial += jnp.dot(inputs, up_ref[...], preferred_element_type=jnp.float32)
        for f in range(cf):
            block = partial[cells * f : cells * (f + 1)].astype(jnp.bfloat16)
            for place, source in enumerate(wanted):
                if source == f:
                    out_ref[place] = block

    return pl.pallas_call(
        body,
        out_shape=jax.ShapeDtypeStruct((len(wanted), cells, w_up.shape[1]), jnp.bfloat16),
        in_specs=[VMEM] * 3 + [ANY],
        out_specs=VMEM,
        compiler_params=limit(2),
        cost_estimate=FREE,
        name="project",
    )(mine, folded, w_up, earlier)


def edge_rows(left, one, two, right, earlier):
    rows, channels, width = one.shape[1:]

    def body(left_ref, one_ref, two_ref, right_ref, *refs):
        pair_ref, next_ref, sems = refs[-3:]
        odd = lax.rem(lax.axis_index("row"), 2)
        frames = (left_ref.at[0], one_ref.at[0], two_ref.at[0], right_ref.at[0])
        moves = []
        for place, frame in enumerate(frames):
            for side, (out, row) in enumerate(((pair_ref, 1 - odd), (next_ref, odd))):
                moves.append(
                    pltpu.make_async_copy(
                        frame.at[row * (rows - 1)], out.at[place], sems.at[2 * place + side]
                    )
                )
        for move in moves:
            move.start()
        for move in moves:
            move.wait()

    shape = jax.ShapeDtypeStruct((4, channels, width), jnp.bfloat16)
    return pl.pallas_call(
        body,
        out_shape=(shape, shape),
        in_specs=[ANY] * (4 + len(earlier)),
        out_specs=(VMEM, VMEM),
        scratch_shapes=[pltpu.SemaphoreType.DMA((8,))],
        compiler_params=limit(2),
        cost_estimate=FREE,
        name="edge_rows",
    )(left, one, two, right, *earlier)


def total(summed):
    def body(summed_ref, out_ref):
        result = summed_ref[0].astype(jnp.float32)
        for source in range(1, summed.shape[0]):
            result += summed_ref[source].astype(jnp.float32)
        out_ref[...] = result.astype(jnp.bfloat16)

    return pl.pallas_call(
        body,
        out_shape=jax.ShapeDtypeStruct(summed.shape[1:], jnp.bfloat16),
        in_specs=[VMEM],
        out_specs=VMEM,
        compiler_params=limit(2),
        cost_estimate=pl.CostEstimate(flops=10000000000, bytes_accessed=0, transcendentals=0),
        name="total",
    )(summed)


def fine_kernel(
    one, two, left_in, right_in, pair_in, next_in, up_own, up_pair, up_near, up_far, one_in, two_in, space, time,
    out, left, right, pair, beyond, gains, stack, second, merged, mixed, turned, sems, out_sems,
):
    channels, width = one.shape[2:]
    cells = 2 * up_own.shape[1]
    row, frame_index = lax.axis_index("row"), lax.axis_index("frame")
    last_row, last_frame = lax.axis_size("row") - 1, lax.axis_size("frame") - 1
    even = lax.rem(row, 2) == 0
    valid_above = (row > 0).astype(jnp.float32)
    valid_below = (row < last_row).astype(jnp.float32)
    valid_beyond = jnp.logical_and(frame_index > 0, frame_index < last_frame).astype(jnp.float32)
    in_time = lax.rem(frame_index, 2) == 1

    def time_of(frame):
        return jnp.where(in_time, frame, 3 - frame)


    moves, leaving = [], []
    halo = ((left_in, left), (right_in, right), (pair_in, pair), (next_in, beyond))
    for place, (source, target) in enumerate(halo):
        moves.append(pltpu.make_async_copy(source, target, sems.at[place]))
    for move in moves:
        move.start()

    for place, gain in enumerate((one_in, two_in)):
        gains[place] = jnp.broadcast_to(0.5 * gain[...].reshape(1, channels), (width, channels)).T
    gain_one, gain_two = gains.at[0], gains.at[1]

    def columns_of(odd):
        cell = lax.broadcasted_iota(jnp.int32, (cells, width), 0) + odd * (cells // 2)
        cell = jnp.where(cell >= cells, cell - cells, cell) * (width // cells)
        column = lax.broadcasted_iota(jnp.int32, (cells, width), 1)
        inside = (column >= cell) & (column < cell + width // cells)
        return inside.astype(jnp.float32).astype(jnp.bfloat16)

    lane = lax.broadcasted_iota(jnp.int32, (channels, width), 1)

    def spread(first, then, expand):
        by_slot = []
        for slot in range(2):
            both = jnp.concatenate(
                [first[slot].astype(jnp.float32), then[slot].astype(jnp.float32)], axis=0
            )
            by_slot.append(
                lax.dot_general(
                    both.astype(jnp.bfloat16),
                    expand,
                    (((0,), (0,)), ((), ())),
                    preferred_element_type=jnp.float32,
                )
            )
        return [by_slot[0]] * 3 + [by_slot[1]]

    def norm(values, gain, scale):
        square = jnp.sum(values * values, axis=0, keepdims=True) * (1.0 / channels)
        inverse = lax.rsqrt(square + 1e-06)
        if scale is not None:
            inverse = inverse * scale
        half = values * inverse * gain[...]
        return half + half * jnp.tanh(half)

    def keep(frame, position, pixels, added, scale):
        total = (pixels.astype(jnp.float32) + added).astype(jnp.bfloat16)
        if frame in (1, 2) and 1 <= position <= 4:
            merged[time_of(frame) - 1, position - 1] = total
        normed = norm(total.astype(jnp.float32), gain_one, scale)
        normed = normed.astype(jnp.bfloat16)
        before = jnp.where(lane == 0, jnp.zeros_like(normed), pltpu.roll(normed, 1, 1))
        after = jnp.where(lane == width - 1, jnp.zeros_like(normed), pltpu.roll(normed, width - 1, 1))
        half, side = ((1, 0), (0, 0), (0, 1), (1, 1))[frame]
        lanes = pl.ds(width * side, width)
        for place, part in enumerate((before, normed, after)):
            stack[half, position, pl.ds(place * channels, channels), lanes] = part

    odd = lax.rem(row, 2)
    here = spread(up_own, up_pair, columns_of(odd))
    further = spread(up_near, up_far, columns_of(1 - odd))
    held = (left.at[0], one.at[0], two.at[0], right.at[0])

    halves = ((1, 2), (0, 3))

    def first_norm(half, position):
        for frame in halves[half]:
            if position == 0:
                pixels = jnp.where(even, beyond[frame], pair[frame])
                added = jnp.where(even, further[frame], here[frame])
                keep(frame, 0, pixels, added, valid_above)
            elif position == 5:
                pixels = jnp.where(even, pair[frame], beyond[frame])
                added = jnp.where(even, here[frame], further[frame])
                keep(frame, 5, pixels, added, valid_below)
            else:
                keep(frame, position, held[frame][position - 1], here[frame], None)

    def convolve(half, row_out):
        window = stack[half, pl.ds(row_out, 3)].reshape(9 * channels, 2 * width)
        return jnp.dot(space[...], window, preferred_element_type=jnp.float32)

    def second_norm(half, row_out, spatial):
        for side in range(2):
            frame = halves[half][side]
            scale = (None, None, None, valid_beyond)[frame]
            normed = norm(spatial[:, side * width : (side + 1) * width], gain_two, scale)
            lanes = pl.ds(width * (row_out % 2), width)
            second[row_out // 2, time_of(frame), :, lanes] = normed.astype(jnp.bfloat16)

    for move in moves:
        move.wait()
    for position in (1, 2, 3):
        first_norm(0, position)
    order = ((0, 1), (0, 2), (0, 0), (0, 3), (1, 1), (1, 2), (1, 0), (1, 3))
    ahead = {
        (0, 1): ((0, 4), (0, 0)),
        (0, 2): ((0, 5), (1, 1)),
        (0, 0): ((1, 2),),
        (0, 3): ((1, 3),),
        (1, 1): ((1, 4), (1, 0)),
        (1, 2): ((1, 5),),
    }
    waiting = None
    for half, row_out in order:
        current = convolve(half, row_out)
        for other in ahead.get((half, row_out), ()):
            first_norm(*other)
        if waiting is not None:
            second_norm(*waiting)
        waiting = (half, row_out, current)
    second_norm(*waiting)

    for frame in range(2):
        for half in range(2):
            window = second[half, pl.ds(frame, 3)].reshape(3 * channels, 2 * width)
            temporal = jnp.dot(time[...], window, preferred_element_type=jnp.float32)
            for side in range(2):
                row_out = 2 * half + side
                sums = merged[frame, row_out].astype(jnp.float32)
                sums += temporal[:, side * width : (side + 1) * width]
                mixed[frame, pl.ds(row_out, channels, stride=4), :] = sums
        turned[frame] = mixed[frame].reshape(channels, 4, width).astype(jnp.bfloat16)
        leave = pltpu.make_async_copy(turned.at[frame], out.at[frame], out_sems.at[frame])
        leave.start()
        leaving.append(leave)
    for leave in leaving:
        leave.wait()


def fine_stage(one, two, left, right, pair, beyond, up_own, up_pair, up_near, up_far, gain_one, gain_two, space, time):
    channels, width = one.shape[2:]
    bf16 = jnp.bfloat16
    copied = (left, right, pair, beyond)
    return pl.pallas_call(
        fine_kernel,
        out_shape=jax.ShapeDtypeStruct((2, channels, 4, width), bf16),
        in_specs=[VMEM] * 2 + [HBM] * 4 + [VMEM] * 8,
        out_specs=HBM,
        scratch_shapes=[pltpu.VMEM(array.shape, array.dtype) for array in copied]
        + [
            pltpu.VMEM((2, channels, width), jnp.float32),
            pltpu.VMEM((2, 6, 3 * channels, 2 * width), bf16),
            pltpu.VMEM((2, 4, channels, 2 * width), bf16),
            pltpu.VMEM((2, 4, channels, width), bf16),
            pltpu.VMEM((2, 4 * channels, width), jnp.float32),
            pltpu.VMEM((2, channels, 4, width), bf16),
            pltpu.SemaphoreType.DMA((len(copied),)),
            pltpu.SemaphoreType.DMA((2,)),
        ],
        compiler_params=limit(28),
        name="fine_stage",
    )(one, two, left, right, pair, beyond, up_own, up_pair, up_near, up_far, gain_one, gain_two, space, time)


def local(fine, coarse, w_qkv, w_out, w_up, gain_one, conv_space, gain_two, conv_time):
    frames = lax.axis_size("frame")
    rows = lax.axis_size("row")
    cf, cells, c_dev = coarse.shape
    fine_c, width = fine.shape[1], fine.shape[3]
    tokens = cf * cells
    share = 8
    groups = [list(range(k, k + share)) for k in range(0, rows, share)]
    partner = [(i, i ^ 1) for i in range(rows)]
    across = [(i, i + 1) for i in range(1, rows - 1, 2)]
    across += [(b, a) for a, b in across]
    beyond = [(i, i + 2) for i in range(0, rows - 2, 2)] + [(i + 2, i) for i in range(1, rows - 2, 2)]

    message = pack(coarse, w_up, share, frames)
    arrived = lax.all_to_all(message, "frame", 0, 0, tiled=True)

    odd_frame = lax.axis_index("frame") % 2
    near_one = jnp.swapaxes(lax.dynamic_slice_in_dim(fine, 1 - odd_frame, 1, 0), 1, 2)
    near_two = jnp.swapaxes(lax.dynamic_slice_in_dim(fine, odd_frame, 1, 0), 1, 2)
    second_pairs = [(i, i + 1) for i in range(1, frames - 1, 2)]
    second_pairs += [(b, a) for a, b in second_pairs]
    beyond_one = lax.ppermute(near_one, "frame", [(i, i ^ 1) for i in range(frames)])
    beyond_two = lax.ppermute(near_two, "frame", second_pairs)

    copies, whole = fold(arrived, w_out, tokens, share)
    folded = lax.all_to_all(copies, "row", 0, 0, tiled=True, axis_index_groups=groups)
    folded = folded.reshape(fine_c, w_out.shape[0])
    conv_space, _ = lax.optimization_barrier((conv_space, copies))
    space = jnp.transpose(conv_space, (3, 0, 1, 2)).reshape(fine_c, 9 * fine_c)
    mine = attend(whole, jnp.swapaxes(w_qkv, 1, 2), coarse)

    per = frames // cf
    wanted = []
    for f in range(frames):
        wanted.append(f // per)
        wanted.append(min(max(f + 2 * (f % 2) - 1, 0), frames - 1) // per)
    outgoing = project(mine, folded, w_up, space, wanted).reshape(frames, 2, cells, fine_c)
    summed = lax.all_to_all(outgoing, "frame", 0, 0, tiled=True)

    conv_time, _ = lax.optimization_barrier((conv_time, outgoing))
    time = jnp.transpose(conv_time, (2, 0, 1)).reshape(fine_c, 3 * fine_c)
    to_pair, to_next = edge_rows(beyond_one, near_one, near_two, beyond_two, (outgoing, time))
    from_pair = lax.ppermute(to_pair, "row", partner)
    from_next = lax.ppermute(to_next, "row", across)

    up_own = total(summed)
    up_pair = lax.ppermute(up_own, "row", partner)
    up_near = lax.ppermute(up_own, "row", across)
    up_far = lax.ppermute(up_own, "row", beyond)
    return fine_stage(
        near_one, near_two, beyond_one, beyond_two, from_pair, from_next, up_own, up_pair, up_near, up_far, gain_one, gain_two, space, time
    )


def solution(mesh):
    return jax.shard_map(
        local,
        mesh=mesh,
        in_specs=(
            P("frame", None, "row", None),
            P(None, "row", "frame"),
            P(None, None, "frame"),
            P("frame", None),
            P("frame", None),
            P(),
            P(),
            P(),
            P(),
        ),
        out_specs=P("frame", None, "row", None),
        check_vma=False,
    )
```

```python
import math

import jax
import jax.numpy as jnp
from jax import lax
from jax.experimental import pallas as pl
from jax.experimental.pallas import tpu as pltpu
from jax.sharding import PartitionSpec as P

HD = 80
VMEM = pl.BlockSpec(memory_space=pltpu.VMEM)
ANY = pl.BlockSpec(memory_space=pl.ANY)
HBM = pl.BlockSpec(memory_space=pltpu.HBM)
FREE = pl.CostEstimate(flops=0, bytes_accessed=0, transcendentals=0)


def limit(mib):
    return pltpu.CompilerParams(vmem_limit_bytes=mib * 2**20)


def pack(coarse, w_up, share, count):
    cf, cells, depth = coarse.shape
    columns = w_up.shape[1] // share

    def body(coarse_in, up_in, out_ref, coarse_ref, up_ref, sems):
        moves = [
            pltpu.make_async_copy(coarse_in, coarse_ref, sems.at[0]),
            pltpu.make_async_copy(up_in, up_ref, sems.at[1]),
        ]
        for move in moves:
            move.start()
        for move in moves:
            move.wait()
        first = lax.rem(lax.axis_index("row"), share) * columns
        shape = (columns, w_up.shape[1])
        wanted = lax.broadcasted_iota(jnp.int32, shape, 0) + first
        pick = (lax.broadcasted_iota(jnp.int32, shape, 1) == wanted).astype(jnp.float32)
        rows = lax.dot_general(
            pick.astype(jnp.bfloat16),
            up_ref[...],
            (((1,), (1,)), ((), ())),
            preferred_element_type=jnp.float32,
        ).astype(jnp.bfloat16)
        for place in range(count):
            for frame in range(cf):
                out_ref[place, pl.ds(frame * cells, cells)] = coarse_ref[frame]
            out_ref[place, pl.ds(cf * cells, columns)] = rows

    return pl.pallas_call(
        body,
        out_shape=jax.ShapeDtypeStruct((count, cf * cells + columns, depth), jnp.bfloat16),
        in_specs=[HBM] * 2,
        out_specs=VMEM,
        scratch_shapes=[
            pltpu.VMEM(coarse.shape, coarse.dtype),
            pltpu.VMEM(w_up.shape, w_up.dtype),
            pltpu.SemaphoreType.DMA((2,)),
        ],
        compiler_params=limit(56),
        cost_estimate=FREE,
        name="pack",
    )(coarse, w_up)


def fold(arrived, w_out, tokens, count):
    blocks, rows, depth = arrived.shape
    heads = w_out.shape[0]

    def body(arrived_ref, out_w_ref, out_ref, cells_ref, whole_ref):
        for block in range(blocks):
            whole_ref[:, pl.ds(block * depth, depth)] = arrived_ref[block]
        cells_ref[...] = whole_ref[pl.ds(0, tokens)]
        total = lax.dot_general(
            whole_ref[pl.ds(tokens, rows - tokens)],
            out_w_ref[...],
            (((1,), (1,)), ((), ())),
            preferred_element_type=jnp.float32,
        ).astype(jnp.bfloat16)
        for place in range(count):
            out_ref[place] = total

    return pl.pallas_call(
        body,
        out_shape=(
            jax.ShapeDtypeStruct((count, rows - tokens, heads), jnp.bfloat16),
            jax.ShapeDtypeStruct((tokens, blocks * depth), jnp.bfloat16),
        ),
        in_specs=[VMEM] * 2,
        out_specs=(VMEM, VMEM),
        scratch_shapes=[pltpu.VMEM((rows, blocks * depth), jnp.bfloat16)],
        compiler_params=limit(2),
        cost_estimate=FREE,
        name="fold",
    )(arrived, w_out)


def attend(whole, w_qkv_t, coarse):
    cf, cells, depth = coarse.shape

    def body(whole_ref, w_ref, coarse_ref, out_ref):
        projected = []
        for part in range(3):
            value = lax.dot_general(
                whole_ref[...],
                w_ref[part],
                (((1,), (1,)), ((), ())),
                preferred_element_type=jnp.float32,
            )
            value = value.astype(jnp.bfloat16).astype(jnp.float32)
            projected.append([value[cells * f : cells * (f + 1)] for f in range(cf)])
        query, keys, values = projected
        for f in range(cf):
            scores = [
                jnp.sum(query[f] * keys[g], axis=1, keepdims=True) * (1.0 / math.sqrt(HD))
                for g in range(cf)
            ]
            most = scores[0]
            for score in scores[1:]:
                most = jnp.maximum(most, score)
            weights = [jnp.exp(score - most) for score in scores]
            total = sum(weights[1:], weights[0])
            mixed = None
            for g in range(cf):
                share = (weights[g] / total).astype(jnp.bfloat16).astype(jnp.float32)
                term = share * values[g]
                mixed = term if mixed is None else mixed + term
            out_ref[0, f] = mixed.astype(jnp.bfloat16)
            out_ref[1, f] = coarse_ref[f]

    return pl.pallas_call(
        body,
        out_shape=jax.ShapeDtypeStruct((2, *coarse.shape), jnp.bfloat16),
        in_specs=[VMEM] * 3,
        out_specs=VMEM,
        compiler_params=limit(2),
        cost_estimate=pl.CostEstimate(flops=10000000000, bytes_accessed=0, transcendentals=0),
        name="attend",
    )(whole, w_qkv_t, coarse)


def project(mine, folded, w_up, earlier, wanted):
    cf, cells, width = mine.shape[1:]

    def body(mine_ref, folded_ref, up_ref, _, out_ref):
        attn = mine_ref[0].reshape(cf * cells, width)
        inputs = mine_ref[1].reshape(cf * cells, width)
        partial = lax.dot_general(
            attn, folded_ref[...], (((1,), (1,)), ((), ())), preferred_element_type=jnp.float32
        )
        partial += jnp.dot(inputs, up_ref[...], preferred_element_type=jnp.float32)
        for f in range(cf):
            block = partial[cells * f : cells * (f + 1)].astype(jnp.bfloat16)
            for place, source in enumerate(wanted):
                if source == f:
                    out_ref[place] = block

    return pl.pallas_call(
        body,
        out_shape=jax.ShapeDtypeStruct((len(wanted), cells, w_up.shape[1]), jnp.bfloat16),
        in_specs=[VMEM] * 3 + [ANY],
        out_specs=VMEM,
        compiler_params=limit(2),
        cost_estimate=FREE,
        name="project",
    )(mine, folded, w_up, earlier)


def edge_rows(left, one, two, right, earlier):
    rows, channels, width = one.shape[1:]

    def body(left_ref, one_ref, two_ref, right_ref, *refs):
        pair_ref, next_ref, sems = refs[-3:]
        odd = lax.rem(lax.axis_index("row"), 2)
        frames = (left_ref.at[0], one_ref.at[0], two_ref.at[0], right_ref.at[0])
        moves = []
        for place, frame in enumerate(frames):
            for side, (out, row) in enumerate(((pair_ref, 1 - odd), (next_ref, odd))):
                moves.append(
                    pltpu.make_async_copy(
                        frame.at[row * (rows - 1)], out.at[place], sems.at[2 * place + side]
                    )
                )
        for move in moves:
            move.start()
        for move in moves:
            move.wait()

    shape = jax.ShapeDtypeStruct((4, channels, width), jnp.bfloat16)
    return pl.pallas_call(
        body,
        out_shape=(shape, shape),
        in_specs=[ANY] * (4 + len(earlier)),
        out_specs=(VMEM, VMEM),
        scratch_shapes=[pltpu.SemaphoreType.DMA((8,))],
        compiler_params=limit(2),
        cost_estimate=FREE,
        name="edge_rows",
    )(left, one, two, right, *earlier)


def total(summed):
    def body(summed_ref, out_ref):
        result = summed_ref[0].astype(jnp.float32)
        for source in range(1, summed.shape[0]):
            result += summed_ref[source].astype(jnp.float32)
        out_ref[...] = result.astype(jnp.bfloat16)

    return pl.pallas_call(
        body,
        out_shape=jax.ShapeDtypeStruct(summed.shape[1:], jnp.bfloat16),
        in_specs=[VMEM],
        out_specs=VMEM,
        compiler_params=limit(2),
        cost_estimate=pl.CostEstimate(flops=10000000000, bytes_accessed=0, transcendentals=0),
        name="total",
    )(summed)


def fine_kernel(
    one, two, left_in, right_in, pair_in, next_in, up_own, up_pair, up_next, one_in, two_in, space, time,
    out, left, right, pair, beyond, gains, stack, second, merged, mixed, turned, sems, out_sems,
):
    channels, width = one.shape[2:]
    cells = 2 * up_own.shape[1]
    row, frame_index = lax.axis_index("row"), lax.axis_index("frame")
    last_row, last_frame = lax.axis_size("row") - 1, lax.axis_size("frame") - 1
    even = lax.rem(row, 2) == 0
    valid_above = (row > 0).astype(jnp.float32)
    valid_below = (row < last_row).astype(jnp.float32)
    valid_beyond = jnp.logical_and(frame_index > 0, frame_index < last_frame).astype(jnp.float32)
    in_time = lax.rem(frame_index, 2) == 1

    def time_of(frame):
        return jnp.where(in_time, frame, 3 - frame)


    moves, leaving = [], []
    halo = ((left_in, left), (right_in, right), (pair_in, pair), (next_in, beyond))
    for place, (source, target) in enumerate(halo):
        moves.append(pltpu.make_async_copy(source, target, sems.at[place]))
    for move in moves:
        move.start()

    for place, gain in enumerate((one_in, two_in)):
        gains[place] = jnp.broadcast_to(0.5 * gain[...].reshape(1, channels), (width, channels)).T
    gain_one, gain_two = gains.at[0], gains.at[1]

    def columns_of(odd):
        cell = lax.broadcasted_iota(jnp.int32, (cells, width), 0) + odd * (cells // 2)
        cell = jnp.where(cell >= cells, cell - cells, cell) * (width // cells)
        column = lax.broadcasted_iota(jnp.int32, (cells, width), 1)
        inside = (column >= cell) & (column < cell + width // cells)
        return inside.astype(jnp.float32).astype(jnp.bfloat16)

    lane = lax.broadcasted_iota(jnp.int32, (channels, width), 1)

    def spread(first, then, expand):
        by_slot = []
        for slot in range(2):
            both = jnp.concatenate(
                [first[slot].astype(jnp.float32), then[slot].astype(jnp.float32)], axis=0
            )
            by_slot.append(
                lax.dot_general(
                    both.astype(jnp.bfloat16),
                    expand,
                    (((0,), (0,)), ((), ())),
                    preferred_element_type=jnp.float32,
                )
            )
        return [by_slot[0]] * 3 + [by_slot[1]]

    def norm(values, gain, scale):
        square = jnp.sum(values * values, axis=0, keepdims=True) * (1.0 / channels)
        inverse = lax.rsqrt(square + 1e-06)
        if scale is not None:
            inverse = inverse * scale
        half = values * inverse * gain[...]
        return half + half * jnp.tanh(half)

    def keep(frame, position, pixels, added, scale):
        total = (pixels.astype(jnp.float32) + added).astype(jnp.bfloat16)
        if frame in (1, 2) and 1 <= position <= 4:
            merged[time_of(frame) - 1, position - 1] = total
        normed = norm(total.astype(jnp.float32), gain_one, scale)
        normed = normed.astype(jnp.bfloat16)
        before = jnp.where(lane == 0, jnp.zeros_like(normed), pltpu.roll(normed, 1, 1))
        after = jnp.where(lane == width - 1, jnp.zeros_like(normed), pltpu.roll(normed, width - 1, 1))
        half, side = ((1, 0), (0, 0), (0, 1), (1, 1))[frame]
        lanes = pl.ds(width * side, width)
        for place, part in enumerate((before, normed, after)):
            stack[half, position, pl.ds(place * channels, channels), lanes] = part

    odd = lax.rem(row, 2)
    here = spread(up_own, up_pair, columns_of(odd))
    further = spread(up_next.at[0], up_next.at[1], columns_of(1 - odd))
    held = (left.at[0], one.at[0], two.at[0], right.at[0])

    halves = ((1, 2), (0, 3))

    def first_norm(half, position):
        for frame in halves[half]:
            if position == 0:
                pixels = jnp.where(even, beyond[frame], pair[frame])
                added = jnp.where(even, further[frame], here[frame])
                keep(frame, 0, pixels, added, valid_above)
            elif position == 5:
                pixels = jnp.where(even, pair[frame], beyond[frame])
                added = jnp.where(even, here[frame], further[frame])
                keep(frame, 5, pixels, added, valid_below)
            else:
                keep(frame, position, held[frame][position - 1], here[frame], None)

    def convolve(half, row_out):
        window = stack[half, pl.ds(row_out, 3)].reshape(9 * channels, 2 * width)
        return jnp.dot(space[...], window, preferred_element_type=jnp.float32)

    def second_norm(half, row_out, spatial):
        for side in range(2):
            frame = halves[half][side]
            scale = (None, None, None, valid_beyond)[frame]
            normed = norm(spatial[:, side * width : (side + 1) * width], gain_two, scale)
            lanes = pl.ds(width * (row_out % 2), width)
            second[row_out // 2, time_of(frame), :, lanes] = normed.astype(jnp.bfloat16)

    for move in moves:
        move.wait()
    for position in (1, 2, 3):
        first_norm(0, position)
    order = ((0, 1), (0, 2), (0, 0), (0, 3), (1, 1), (1, 2), (1, 0), (1, 3))
    ahead = {
        (0, 1): ((0, 4), (0, 0)),
        (0, 2): ((0, 5), (1, 1)),
        (0, 0): ((1, 2),),
        (0, 3): ((1, 3),),
        (1, 1): ((1, 4), (1, 0)),
        (1, 2): ((1, 5),),
    }
    waiting = None
    for half, row_out in order:
        current = convolve(half, row_out)
        for other in ahead.get((half, row_out), ()):
            first_norm(*other)
        if waiting is not None:
            second_norm(*waiting)
        waiting = (half, row_out, current)
    second_norm(*waiting)

    for frame in range(2):
        for half in range(2):
            window = second[half, pl.ds(frame, 3)].reshape(3 * channels, 2 * width)
            temporal = jnp.dot(time[...], window, preferred_element_type=jnp.float32)
            for side in range(2):
                row_out = 2 * half + side
                sums = merged[frame, row_out].astype(jnp.float32)
                sums += temporal[:, side * width : (side + 1) * width]
                mixed[frame, pl.ds(row_out, channels, stride=4), :] = sums
        turned[frame] = mixed[frame].reshape(channels, 4, width).astype(jnp.bfloat16)
        leave = pltpu.make_async_copy(turned.at[frame], out.at[frame], out_sems.at[frame])
        leave.start()
        leaving.append(leave)
    for leave in leaving:
        leave.wait()


def fine_stage(one, two, left, right, pair, beyond, up_own, up_pair, up_next, gain_one, gain_two, space, time):
    channels, width = one.shape[2:]
    bf16 = jnp.bfloat16
    copied = (left, right, pair, beyond)
    return pl.pallas_call(
        fine_kernel,
        out_shape=jax.ShapeDtypeStruct((2, channels, 4, width), bf16),
        in_specs=[VMEM] * 2 + [HBM] * 4 + [VMEM] * 7,
        out_specs=HBM,
        scratch_shapes=[pltpu.VMEM(array.shape, array.dtype) for array in copied]
        + [
            pltpu.VMEM((2, channels, width), jnp.float32),
            pltpu.VMEM((2, 6, 3 * channels, 2 * width), bf16),
            pltpu.VMEM((2, 4, channels, 2 * width), bf16),
            pltpu.VMEM((2, 4, channels, width), bf16),
            pltpu.VMEM((2, 4 * channels, width), jnp.float32),
            pltpu.VMEM((2, channels, 4, width), bf16),
            pltpu.SemaphoreType.DMA((len(copied),)),
            pltpu.SemaphoreType.DMA((2,)),
        ],
        compiler_params=limit(28),
        name="fine_stage",
    )(one, two, left, right, pair, beyond, up_own, up_pair, up_next, gain_one, gain_two, space, time)


def local(fine, coarse, w_qkv, w_out, w_up, gain_one, conv_space, gain_two, conv_time):
    frames = lax.axis_size("frame")
    rows = lax.axis_size("row")
    cf, cells, c_dev = coarse.shape
    fine_c, width = fine.shape[1], fine.shape[3]
    tokens = cf * cells
    share = 8
    groups = [list(range(k, k + share)) for k in range(0, rows, share)]
    partner = [(i, i ^ 1) for i in range(rows)]
    across = [(i, i + 1) for i in range(1, rows - 1, 2)]
    across += [(b, a) for a, b in across]

    message = pack(coarse, w_up, share, frames)
    arrived = lax.all_to_all(message, "frame", 0, 0, tiled=True)

    odd_frame = lax.axis_index("frame") % 2
    near_one = jnp.swapaxes(lax.dynamic_slice_in_dim(fine, 1 - odd_frame, 1, 0), 1, 2)
    near_two = jnp.swapaxes(lax.dynamic_slice_in_dim(fine, odd_frame, 1, 0), 1, 2)
    second_pairs = [(i, i + 1) for i in range(1, frames - 1, 2)]
    second_pairs += [(b, a) for a, b in second_pairs]
    beyond_one = lax.ppermute(near_one, "frame", [(i, i ^ 1) for i in range(frames)])
    beyond_two = lax.ppermute(near_two, "frame", second_pairs)

    copies, whole = fold(arrived, w_out, tokens, share)
    folded = lax.all_to_all(copies, "row", 0, 0, tiled=True, axis_index_groups=groups)
    folded = folded.reshape(fine_c, w_out.shape[0])
    conv_space, _ = lax.optimization_barrier((conv_space, copies))
    space = jnp.transpose(conv_space, (3, 0, 1, 2)).reshape(fine_c, 9 * fine_c)
    mine = attend(whole, jnp.swapaxes(w_qkv, 1, 2), coarse)

    per = frames // cf
    wanted = []
    for f in range(frames):
        wanted.append(f // per)
        wanted.append(min(max(f + 2 * (f % 2) - 1, 0), frames - 1) // per)
    outgoing = project(mine, folded, w_up, space, wanted).reshape(frames, 2, cells, fine_c)
    summed = lax.all_to_all(outgoing, "frame", 0, 0, tiled=True)

    conv_time, _ = lax.optimization_barrier((conv_time, outgoing))
    time = jnp.transpose(conv_time, (2, 0, 1)).reshape(fine_c, 3 * fine_c)
    to_pair, to_next = edge_rows(beyond_one, near_one, near_two, beyond_two, (outgoing, time))
    from_pair = lax.ppermute(to_pair, "row", partner)
    from_next = lax.ppermute(to_next, "row", across)

    up_own = total(summed)
    up_pair = lax.ppermute(up_own, "row", partner)
    up_next = lax.ppermute(jnp.stack([up_own, up_pair]), "row", across)
    return fine_stage(
        near_one, near_two, beyond_one, beyond_two, from_pair, from_next, up_own, up_pair, up_next, gain_one, gain_two, space, time
    )


def solution(mesh):
    return jax.shard_map(
        local,
        mesh=mesh,
        in_specs=(
            P("frame", None, "row", None),
            P(None, "row", "frame"),
            P(None, None, "frame"),
            P("frame", None),
            P("frame", None),
            P(),
            P(),
            P(),
            P(),
        ),
        out_specs=P("frame", None, "row", None),
        check_vma=False,
    )
```
